128 devices in a mesh: req: 16 (over x_hi, y, core), tensor: 8 (over x_lo, z).
Axes of the slice: x: 4 (x_hi: 2, x_lo: 2; x = x_hi * 2 + x_lo), y: 4, z: 4, core: 2. Of those that a mesh axis runs over, the one named last changes fastest.
Arguments:
- hidden: bfloat16 [32, 512, 1792], P('req', 'tensor')
- suffix_len: int32 [32], P('req'), may hold values from 1 to 512, as said below
- request_group: int32 [32], P('req'), may hold values from 0 to 63
- group_slot: int32 [64], replicated, may hold values from 0 to 63, each once
- norm_first: float32 [1792], replicated, may hold values from 0.5 to 2
- query_weight: bfloat16 [1792, 256], P(None, 'tensor'), may hold values from -0.125 to 0.125
- key_weight: bfloat16 [1792, 256], P(None, 'tensor'), may hold values from -0.125 to 0.125
- value_weight: bfloat16 [1792, 1792], P(None, 'tensor'), may hold values from -0.125 to 0.125
- filter_gate: bfloat16 [1792, 1792], P(None, 'tensor'), may hold values from -0.125 to 0.125
- filter_taps: float32 [3, 1792], P(None, 'tensor'), may hold values from -3 to 3
- linear_out: bfloat16 [1792, 1792], P('tensor'), may hold values from -0.125 to 0.125
- norm_second: float32 [1792], replicated, may hold values from 0.5 to 1.5
- window_query: bfloat16 [1792, 1792], P(None, 'tensor')
- window_key: bfloat16 [1792, 1792], P(None, 'tensor')
- window_value: bfloat16 [1792, 1792], P(None, 'tensor'), may hold values from -0.125 to 0.125
- window_out: bfloat16 [1792, 1792], P('tensor'), may hold values from -0.125 to 0.125
- norm_third: float32 [1792], replicated, may hold values from 0.5 to 1.5
- gate_weight: bfloat16 [1792, 7168], P(None, 'tensor'), may hold values from -0.125 to 0.125
- up_weight: bfloat16 [1792, 7168], P(None, 'tensor'), may hold values from -0.125 to 0.125
- down_weight: bfloat16 [7168, 1792], P('tensor'), may hold values from -0.0625 to 0.0625
- prefix_sums: float32 [64, 16, 273, 112], P('req', 'tensor'), as said below
- prefix_norms: float32 [64, 16, 273], P('req', 'tensor'), as said below
- prefix_keys: bfloat16 [64, 64, 1792], P('req', None, 'tensor'), may hold values from -6 to 6
- prefix_values: bfloat16 [64, 64, 1792], P('req', None, 'tensor'), may hold values from -6 to 6
- prefix_tail: bfloat16 [64, 2, 1792], P('req', None, 'tensor'), may hold values from -10 to 10
Outputs:
- hidden_out: bfloat16 [32, 512, 1792], P('req', 'tensor')
- final_norm: float32 [32], P('req')
- top_logit: float32 [32], P('req')
The draws below stay inside these ranges and needn't reach their ends.
Inputs may be any that keep to these rules, and one draw needn't show every extreme that they name: `suffix_len`: each request's suffix is either a short one of at most 32 tokens or a long one of more than 384; some request has exactly 512. `group_slot`: each slot holds exactly one group. `prefix_sums`: A sum over 128 prefix tokens of the key feature map times the value. `prefix_norms`: A sum over the same 128 tokens of the key feature map, so its inner product with any feature map is positive.
All inputs are finite; a program needn't handle non-finite values.
Results may differ from the reference program's by a relative error of at most 0.024.
Values may be sent and summed in bfloat16 or wider, within the bound.
A program may use at most 128 MiB of HBM per device.

```python
import math
import jax
import jax.numpy as jnp
from jax import lax

D = 1792
LH = 16
FD = 16
HS = 112
SH = 16
FF = 7168
WIN = 64
KC = 3
PREFIX = 128
LMAX = 512
REQS = 32
SLOTS = 64
GROUPS = 64
N_TENSOR = 8


def features_drawn(vectors):
    floats = vectors.astype(jnp.float32)
    dimension = floats.shape[-1]
    constant = jnp.ones(floats.shape[:-1] + (1,), jnp.float32)
    linear_part = floats * dimension ** (-0.25)
    square_part = (floats[..., :, None] * floats[..., None, :]).reshape(floats.shape[:-1] + (dimension * dimension,))
    square_part = square_part * (2.0 * dimension) ** (-0.5)
    return jnp.concatenate([constant, linear_part, square_part], axis=-1)


def prefix_terms(key):
    key_draw, value_draw, scale_draw = jax.random.split(jax.random.fold_in(key, 11), 3)
    head_scale = jnp.exp(jax.random.uniform(scale_draw, (SLOTS, LH, 1, 1), jnp.float32, -0.6931, 0.6931))
    past_keys = jax.random.normal(key_draw, (SLOTS, LH, PREFIX, FD), jnp.float32) * head_scale
    past_values = jax.random.normal(value_draw, (SLOTS, LH, PREFIX, HS), jnp.float32)
    mapped = features_drawn(past_keys)
    state_sums = jnp.einsum('ahpf,ahpd->ahfd', mapped, past_values, precision=lax.Precision.HIGHEST)
    return (state_sums, jnp.sum(mapped, axis=2))


def draw_prefix_sums(key, part):
    state_sums, state_norms = prefix_terms(key)
    return state_sums


def draw_prefix_norms(key, part):
    state_sums, state_norms = prefix_terms(key)
    return state_norms


def draw_suffix_len(key, part):
    kind_key, short_key, long_key, pick_key = jax.random.split(jax.random.fold_in(key, 23), 4)
    longish = jax.random.randint(kind_key, (REQS,), 0, 2)
    short_len = jax.random.randint(short_key, (REQS,), 1, LMAX // 16 + 1)
    long_len = LMAX - jax.random.randint(long_key, (REQS,), 0, LMAX // 4)
    picked = jax.random.randint(pick_key, (), 0, REQS)
    lengths = jnp.where(longish == 1, long_len, short_len)
    return jnp.where(jnp.arange(REQS) == picked, LMAX, lengths).astype(jnp.int32)


def draw_hidden(key, part):
    base_key = jax.random.fold_in(jax.random.fold_in(key, 41), 0)
    rows = jax.random.truncated_normal(base_key, -6.0, 6.0, (REQS, LMAX, D), jnp.float32)
    return rows.astype(jnp.bfloat16)


def window_pair(key):
    query_key, own_key = jax.random.split(jax.random.fold_in(key, 31), 2)
    scale = D ** (-0.5)
    query_part = jax.random.truncated_normal(query_key, -4.0, 4.0, (D, SH * HS), jnp.float32) * scale
    own_part = jax.random.truncated_normal(own_key, -4.0, 4.0, (D, SH * HS), jnp.float32) * scale
    key_part = own_part
    return (query_part, key_part)


def draw_window_query(key, part):
    query_part, key_part = window_pair(key)
    return query_part.astype(jnp.bfloat16)


def draw_window_key(key, part):
    query_part, key_part = window_pair(key)
    return key_part.astype(jnp.bfloat16)


def with_ends(entries, key, low, high):
    longest = entries.shape.index(max(entries.shape))
    spots = []
    for shift in (0, 1):
        where = [jax.random.randint(jax.random.fold_in(key, axis), (), 0, length) for axis, length in enumerate(entries.shape)]
        where[longest] = (where[longest] + shift) % entries.shape[longest]
        spots.append(tuple(where))
    return entries.at[spots[0]].set(low).at[spots[1]].set(high)


def shard_levels(stream_key, shape, shards, least, high):
    gain = 1.0
    for dim, shards_of in shards:
        draws = jax.random.uniform(jax.random.fold_in(jax.random.fold_in(stream_key, 6), dim), (shards_of,), jnp.float32, least / len(shards), high / len(shards))
        gain = gain * jnp.repeat(jnp.exp(draws), shape[dim] // shards_of).reshape((-1,) + (1,) * (len(shape) - 1 - dim))
    return gain


def normal_values(stream_key, shape, scale, bound, cuts=(), dtype=jnp.bfloat16):
    gain = shard_levels(stream_key, shape, cuts, -0.22, 0.18) if cuts else 1.0
    array = jax.random.normal(stream_key, shape, jnp.float32) * scale * gain
    return jnp.minimum(jnp.maximum(array, -bound), bound).astype(dtype)


def setup_inputs(seed: int = 0) -> dict:
    key_list = jax.random.split(jax.random.key(seed), 26)
    hidden = draw_hidden(jax.random.fold_in(key_list[25], 71), 0)
    suffix_len = draw_suffix_len(jax.random.fold_in(key_list[25], 71), 0)
    request_group = with_ends(jax.random.randint(key_list[2], (REQS,), 0, GROUPS), jax.random.fold_in(key_list[2], 1), 0, GROUPS - 1).astype(jnp.int32)
    group_slot = jax.random.permutation(key_list[3], GROUPS).astype(jnp.int32)
    norm_first = jnp.clip(jnp.exp(jax.random.uniform(key_list[4], (D,), jnp.float32, math.log(0.5), math.log(2.0))), 0.5, 2.0)
    query_weight = normal_values(key_list[5], (D, LH * FD), D ** -0.5, 0.125, ((1, 8),))
    key_weight = normal_values(key_list[6], (D, LH * FD), D ** -0.5, 0.125, ((1, 8),))
    value_weight = normal_values(key_list[7], (D, LH * HS), D ** -0.5, 0.125, ((1, 8),))
    filter_gate = normal_values(key_list[8], (D, LH * HS), D ** -0.5, 0.125, ((1, 8),))
    filter_taps = normal_values(key_list[9], (KC, LH * HS), 0.6, 3.0, ((1, 8),), jnp.float32)
    linear_out = normal_values(key_list[10], (LH * HS, D), (LH * HS) ** -0.5, 0.125, ((0, 8),))
    norm_second = jnp.clip(1.0 + 0.1 * jax.random.normal(key_list[11], (D,), jnp.float32), 0.5, 1.5)
    window_query = draw_window_query(jax.random.fold_in(key_list[25], 71), 0)
    window_key = draw_window_key(jax.random.fold_in(key_list[25], 71), 0)
    window_value = normal_values(key_list[14], (D, SH * HS), D ** -0.5, 0.125, ((1, 8),))
    window_out = normal_values(key_list[15], (SH * HS, D), (SH * HS) ** -0.5, 0.125, ((0, 8),))
    norm_third = jnp.clip(1.0 + 0.1 * jax.random.normal(key_list[16], (D,), jnp.float32), 0.5, 1.5)
    gate_weight = normal_values(key_list[17], (D, FF), D ** -0.5, 0.125, ((1, 8),))
    up_weight = normal_values(key_list[18], (D, FF), D ** -0.5, 0.125, ((1, 8),))
    down_weight = normal_values(key_list[19], (FF, D), FF ** -0.5, 0.0625, ((0, 8),))
    prefix_sums = draw_prefix_sums(jax.random.fold_in(key_list[25], 71), 0)
    prefix_norms = draw_prefix_norms(jax.random.fold_in(key_list[25], 71), 0)
    prefix_keys = normal_values(key_list[22], (SLOTS, WIN, SH * HS), 1.0, 6.0, ((0, 16), (2, 8)))
    prefix_values = normal_values(key_list[23], (SLOTS, WIN, SH * HS), 1.0, 6.0, ((0, 16), (2, 8)))
    prefix_tail = normal_values(key_list[24], (SLOTS, KC - 1, LH * HS), 2.0, 10.0, ((0, 16), (2, 8)))
    return {"hidden": hidden, "suffix_len": suffix_len, "request_group": request_group, "group_slot": group_slot, "norm_first": norm_first, "query_weight": query_weight, "key_weight": key_weight, "value_weight": value_weight, "filter_gate": filter_gate, "filter_taps": filter_taps, "linear_out": linear_out, "norm_second": norm_second, "window_query": window_query, "window_key": window_key, "window_value": window_value, "window_out": window_out, "norm_third": norm_third, "gate_weight": gate_weight, "up_weight": up_weight, "down_weight": down_weight, "prefix_sums": prefix_sums, "prefix_norms": prefix_norms, "prefix_keys": prefix_keys, "prefix_values": prefix_values, "prefix_tail": prefix_tail}


EPS = 1e-05

def rms_norm(row_block, gain_vector):
    floats = row_block.astype(jnp.float32)
    inverse_rms = lax.rsqrt(lax.optimization_barrier(jnp.mean(floats * floats, axis=-1, keepdims=True)) + EPS)
    return (floats * inverse_rms * gain_vector.astype(jnp.float32)).astype(jnp.bfloat16)

def features(vectors):
    floats = vectors.astype(jnp.float32)
    dimension = floats.shape[-1]
    constant = jnp.ones(floats.shape[:-1] + (1,), jnp.float32)
    linear_part = floats * dimension ** (-0.25)
    square_part = (floats[..., :, None] * floats[..., None, :]).reshape(floats.shape[:-1] + (dimension * dimension,))
    square_part = square_part * (2.0 * dimension) ** (-0.5)
    return jnp.concatenate([constant, linear_part, square_part], axis=-1)

def rounded(values):
    return lax.optimization_barrier(values.astype(jnp.bfloat16)).astype(jnp.float32)

def tensor_sum(left_rows, right_matrix):
    row_total, inner_total = left_rows.shape
    share_size = inner_total // N_TENSOR
    pieces = left_rows.astype(jnp.float32).reshape(row_total, N_TENSOR, share_size)
    blocks = right_matrix.astype(jnp.float32).reshape(N_TENSOR, share_size, right_matrix.shape[1])
    partial_sum = jnp.einsum('rnk,nkd->nrd', pieces, blocks)
    return lax.optimization_barrier(jnp.sum(rounded(partial_sum), axis=0))

def reference(hidden, suffix_len, request_group, group_slot, norm_first, query_weight, key_weight, value_weight, filter_gate, filter_taps, linear_out, norm_second, window_query, window_key, window_value, window_out, norm_third, gate_weight, up_weight, down_weight, prefix_sums, prefix_norms, prefix_keys, prefix_values, prefix_tail):
    slot_ids = group_slot[request_group].astype(jnp.int32)
    position = jnp.arange(LMAX)
    causal = position[:, None] >= position[None, :]
    key_place = jnp.arange(WIN + LMAX)
    allowed = (key_place[None, :] > position[:, None]) & (key_place[None, :] <= position[:, None] + WIN)

    def one_request(request):
        row_block, length, slot_index = request
        normed = rms_norm(row_block, norm_first)
        queries = jnp.dot(normed, query_weight, preferred_element_type=jnp.float32).astype(jnp.bfloat16).reshape(LMAX, LH, FD)
        key_rows = jnp.dot(normed, key_weight, preferred_element_type=jnp.float32).astype(jnp.bfloat16).reshape(LMAX, LH, FD)
        values_lin = jnp.dot(normed, value_weight, preferred_element_type=jnp.float32).astype(jnp.bfloat16)
        gating = jnp.dot(normed, filter_gate, preferred_element_type=jnp.float32).astype(jnp.bfloat16)
        extended = jnp.concatenate([prefix_tail[slot_index], values_lin], axis=0).astype(jnp.float32)
        convolved = sum((filter_taps[offset] * extended[KC - 1 - offset:KC - 1 - offset + LMAX] for offset in range(KC)))
        mixed_values = (convolved * jax.nn.silu(gating.astype(jnp.float32))).astype(jnp.bfloat16).reshape(LMAX, LH, HS)
        scores = jnp.einsum('thf,shf->hts', queries.astype(jnp.float32), key_rows.astype(jnp.float32)) * FD ** (-0.5)
        weights_lin = jnp.where(causal[None], 1.0 + scores + 0.5 * scores * scores, 0.0)
        numerator = jnp.einsum('hts,shd->thd', rounded(weights_lin), mixed_values.astype(jnp.float32))
        denominator = jnp.transpose(lax.optimization_barrier(jnp.sum(weights_lin, axis=-1)))
        mapped = features(queries)
        numerator = numerator + jnp.einsum('thf,hfd->thd', mapped, prefix_sums[slot_index], precision=lax.Precision.HIGHEST)
        denominator = denominator + jnp.einsum('thf,hf->th', mapped, prefix_norms[slot_index], precision=lax.Precision.HIGHEST)
        linear_rows = (numerator / denominator[..., None]).astype(jnp.bfloat16).reshape(LMAX, LH * HS)
        first_out = (row_block.astype(jnp.float32) + tensor_sum(linear_rows, linear_out)).astype(jnp.bfloat16)
        normed = rms_norm(first_out, norm_second)
        window_q = jnp.dot(normed, window_query, preferred_element_type=jnp.float32).astype(jnp.bfloat16).reshape(LMAX, SH, HS)
        window_k = jnp.dot(normed, window_key, preferred_element_type=jnp.float32).astype(jnp.bfloat16)
        window_v = jnp.dot(normed, window_value, preferred_element_type=jnp.float32).astype(jnp.bfloat16)
        all_keys = jnp.concatenate([prefix_keys[slot_index], window_k], axis=0).reshape(WIN + LMAX, SH, HS)
        all_values = jnp.concatenate([prefix_values[slot_index], window_v], axis=0).reshape(WIN + LMAX, SH, HS)
        logits = jnp.einsum('thd,phd->htp', window_q.astype(jnp.float32), all_keys.astype(jnp.float32)) * HS ** (-0.5)
        logits = jnp.where(allowed[None], logits, -jnp.inf)
        row_max = lax.optimization_barrier(jnp.max(logits, axis=-1, keepdims=True))
        exponent = jnp.exp(logits - row_max)
        probabilities = (exponent / lax.optimization_barrier(jnp.sum(exponent, axis=-1, keepdims=True))).astype(jnp.bfloat16)
        attended = jnp.einsum('htp,phd->thd', probabilities.astype(jnp.float32), all_values.astype(jnp.float32)).astype(jnp.bfloat16).reshape(LMAX, SH * HS)
        second_out = (first_out.astype(jnp.float32) + tensor_sum(attended, window_out)).astype(jnp.bfloat16)
        final_mask = position == length - 1
        best_logit = jnp.max(jnp.where(final_mask[None, :], row_max[..., 0], -jnp.inf))
        normed = rms_norm(second_out, norm_third)
        gate_rows = jnp.dot(normed, gate_weight, preferred_element_type=jnp.float32)
        up_rows = jnp.dot(normed, up_weight, preferred_element_type=jnp.float32)
        inner_rows = (jax.nn.silu(gate_rows) * up_rows).astype(jnp.bfloat16)
        third_out = (second_out.astype(jnp.float32) + tensor_sum(inner_rows, down_weight)).astype(jnp.bfloat16)
        live = position < length
        masked = jnp.where(live[:, None], third_out, jnp.zeros_like(third_out))
        third_f = third_out.astype(jnp.float32)
        squares = jnp.sum(jnp.where(live[:, None], third_f * third_f, 0.0))
        row_norm = jnp.sqrt(squares / D)
        return (masked, row_norm, best_logit)
    hidden_out, final_norm, top_logit = lax.map(one_request, (hidden, suffix_len, slot_ids))
    return (hidden_out, final_norm, top_logit)
```

```python
import functools

import jax
import jax.numpy as jnp
import numpy as np
from jax import lax
from jax.experimental import pallas as pl
from jax.experimental.pallas import tpu as pltpu
from jax.sharding import PartitionSpec as P

D = 1792
FD = 16
HS = 112
WIN = 64
LMAX = 512
ROWS = 64
FFL = 896
PF = 160
EPS = 1e-05
BF = jnp.bfloat16
F32 = jnp.float32
MESH = pl.DeviceIdType.MESH
HALVES = ((0, 896), (896, 896))
THIRDS = ((0, 640), (640, 640), (1280, 512))


def constants():
    pairs = [(i, j) for i in range(FD) for j in range(i, FD)]
    fold = np.zeros((PF, 273), np.float32)
    left = np.zeros((2, 256, 256), np.float32)
    right = np.zeros((2, 256, 256), np.float32)
    rows = np.zeros((8, 256), np.float32)
    fold[0, 0] = 1.0
    rows[0, 0] = 1.0
    rows[1, 0] = 1.0
    rows[2, 0] = 1.0
    for i in range(FD):
        fold[1 + i, 1 + i] = 1.0
        for h in range(2):
            left[h, 224 + 16 * h + i, 1 + i] = 1.0
        rows[1, 1 + i] = 1.0
        rows[2, 1 + i] = FD ** (-0.25)
    for n, (i, j) in enumerate(pairs):
        fold[17 + n, 17 + FD * i + j] = 1.0
        fold[17 + n, 17 + FD * j + i] = 1.0
        for h in range(2):
            left[h, 224 + 16 * h + i, 17 + n] = 1.0
            right[h, 224 + 16 * h + j, 17 + n] = 1.0
        rows[2, 17 + n] = (2.0 * FD) ** (-0.5)
    place = np.zeros((3, 112, 256), np.float32)
    for h in range(2):
        for d in range(HS):
            place[h, d, HS * h + d] = 1.0
    norm_place = np.zeros((4, 8, 256), np.float32)
    for s in range(4):
        for h in range(2):
            norm_place[s, 2 * s + h, 224 + h] = 1.0
    tail_place = np.zeros((PF, 8), np.float32)
    tail_place[158, 0] = 1.0
    tail_place[159, 1] = 1.0
    return (
        jnp.asarray(fold, BF),
        jnp.asarray(left, BF),
        jnp.asarray(right, BF),
        jnp.asarray(rows, F32),
        jnp.asarray(place[:2], BF),
        jnp.asarray(norm_place, BF),
        jnp.asarray(tail_place, BF),
    )


def dot(a, b):
    return jnp.dot(a, b, preferred_element_type=F32)


def dot_t(a, b):
    return lax.dot_general(a, b, (((1,), (1,)), ((), ())), preferred_element_type=F32)


def ds(start, size):
    return pl.ds(pl.multiple_of(start, 16), size)


def kernel(
    ids_ref,
    hidden_ref,
    gains_ref,
    taps_ref,
    info_ref,
    sums_ref,
    norms_ref,
    tail_ref,
    fold_ref,
    left_ref,
    right_ref,
    frow_ref,
    place_ref,
    nplace_ref,
    tplace_ref,
    keys_hbm,
    values_hbm,
    qw_hbm,
    kw_hbm,
    vw_hbm,
    uw_hbm,
    lo_hbm,
    wq_hbm,
    wk_hbm,
    wv_hbm,
    wo_hbm,
    gate_hbm,
    up_hbm,
    down_hbm,
    out_ref,
    scal_ref,
    qw,
    kw,
    vw,
    uw,
    wvq,
    wuk,
    lo,
    wq,
    wk,
    wv,
    wo,
    gate,
    up,
    down,
    xg,
    pb,
    l0,
    l1,
    l2,
    res,
    ys,
    ykv,
    sels,
    selkv,
    rcvs,
    rcvkv,
    sfin,
    kvfin,
    idr,
    ids_smem,
    vqb,
    ukb,
    vf,
    m1,
    ybuf,
    qbuf,
    kbuf,
    vbuf,
    fbuf,
    topbuf,
    fin,
    fins,
    wsem,
    ag_s,
    ag_r,
    rs_s,
    rs_r,
    pf_s,
    pf_r,
    sel_s,
    sel_r,
    fin_s,
    fin_r,
    loc,
):
    t = lax.axis_index("tensor")
    rq = lax.axis_index("req")
    z = lax.rem(t, 4)
    xl = t // 4
    core = lax.rem(rq, 2)
    y = lax.rem(rq // 2, 4)
    xh = rq // 8

    def tdev(dx, dz):
        return lax.rem(xl + dx, 2) * 4 + lax.rem(z + dz, 4)

    b_me, b_zp, b_zm, b_zz = tdev(0, 0), tdev(0, 1), tdev(0, 3), tdev(0, 2)
    b_xp, b_xzp, b_xzm, b_xzz = tdev(1, 0), tdev(1, 1), tdev(1, 3), tdev(1, 2)
    y_up = xh * 8 + lax.rem(y + 1, 4) * 2 + core
    y_dn = xh * 8 + lax.rem(y + 3, 4) * 2 + core
    pals = [
        lax.rem(xh + dx, 2) * 8 + y * 2 + lax.rem(core + dc, 2)
        for dx, dc in ((0, 1), (1, 0), (1, 1))
    ]

    barrier = pltpu.get_barrier_semaphore()
    for k in range(1, 8):
        pl.semaphore_signal(
            barrier, inc=1, device_id={"tensor": lax.rem(t + k, 8)}, device_id_type=MESH
        )
    for other in [y_up, y_dn] + pals:
        pl.semaphore_signal(barrier, inc=1, device_id={"req": other}, device_id_type=MESH)

    weights = [
        (vw_hbm, vw),
        (qw_hbm, qw),
        (uw_hbm, uw),
        (kw_hbm, kw),
        (lo_hbm, lo.at[pl.ds(0, 224)]),
        (wq_hbm, wq),
        (wk_hbm, wk),
        (wv_hbm, wv),
        (wo_hbm, wo),
        (gate_hbm, gate),
        (up_hbm, up),
        (down_hbm, down),
    ]
    kv_loads = [
        pltpu.make_async_copy(keys_hbm, ykv.at[y, :, pl.ds(0, 64), :], loc.at[0]),
        pltpu.make_async_copy(values_hbm, ykv.at[y, :, pl.ds(64, 64), :], loc.at[1]),
    ]
    for c in kv_loads:
        c.start()
    loads = [
        pltpu.make_async_copy(src, dst, wsem.at[n]) for n, (src, dst) in enumerate(weights)
    ]
    for c in loads:
        c.start()

    def rows(b):
        return pl.ds(pl.multiple_of(b * ROWS, ROWS), ROWS)

    def remote(src, dst, ssem, rsem, to):
        return pltpu.make_async_remote_copy(
            src_ref=src, dst_ref=dst, send_sem=ssem, recv_sem=rsem, device_id=to,
            device_id_type=MESH,
        )

    def ag_copies(ph, r, lo_n=0, hi_n=12):
        g = xg.at[ph, r]
        plan = [
            (b_me, (0, D), b_zp),
            (b_me, (0, D), b_zm),
            (b_me, (0, D), b_xp),
            (b_zm, HALVES[0], b_zp),
            (b_zp, HALVES[1], b_zm),
            (b_zm, HALVES[0], b_xp),
            (b_zp, HALVES[0], b_xp),
            (b_xp, HALVES[1], b_zp),
            (b_xp, HALVES[1], b_zm),
            (b_zz, THIRDS[0], b_xp),
            (b_xzm, THIRDS[1], b_zp),
            (b_xzp, THIRDS[2], b_zm),
        ]
        return [
            remote(
                g.at[rows(b), pl.ds(*lanes)], g.at[rows(b), pl.ds(*lanes)],
                ag_s.at[r, n], ag_r.at[r, n], {"tensor": to},
            )
            for n, (b, lanes, to) in enumerate(plan)
            if lo_n <= n < hi_n
        ]

    def ag_waits(ph, r, lo_n, hi_n):
        g = xg.at[ph, r]
        got = [
            (b_zm, (0, D)),
            (b_zp, (0, D)),
            (b_xp, (0, D)),
            (b_zz, HALVES[0]),
            (b_zz, HALVES[1]),
            (b_xzm, HALVES[0]),
            (b_xzp, HALVES[0]),
            (b_xzm, HALVES[1]),
            (b_xzp, HALVES[1]),
            (b_xzz, THIRDS[0]),
            (b_xzz, THIRDS[1]),
            (b_xzz, THIRDS[2]),
        ]
        return [
            remote(
                g.at[rows(b), pl.ds(*lanes)], g.at[rows(b), pl.ds(*lanes)],
                ag_s.at[r, n], ag_r.at[r, n], {"tensor": b_xp},
            )
            for n, (b, lanes) in enumerate(got)
            if lo_n <= n < hi_n
        ]

    def ag0(ph, r):
        for c in ag_copies(ph, r, 0, 3):
            c.start()

    def ag1(ph, r):
        for c in ag_waits(ph, r, 0, 3):
            c.wait_recv()
        for c in ag_copies(ph, r, 3, 9):
            c.start()

    def ag2(ph, r):
        for c in ag_waits(ph, r, 3, 9):
            c.wait_recv()
        for c in ag_copies(ph, r, 9, 12):
            c.start()

    def agf(ph, r):
        for c in ag_waits(ph, r, 9, 12):
            c.wait_recv()
        for c in ag_copies(ph, r):
            c.wait_send()

    def rs_copies(r, lo_n=0, hi_n=12):
        p = pb.at[r]
        plan = [
            (b_xzz, THIRDS[0], b_xp, l0.at[r, :, pl.ds(*THIRDS[0])]),
            (b_xzz, THIRDS[1], b_zm, l0.at[r, :, pl.ds(*THIRDS[1])]),
            (b_xzz, THIRDS[2], b_zp, l0.at[r, :, pl.ds(*THIRDS[2])]),
            (b_zz, HALVES[0], b_zm, l1.at[r, 0]),
            (b_zz, HALVES[1], b_zp, l1.at[r, 1]),
            (b_xzm, HALVES[0], b_xp, l1.at[r, 2]),
            (b_xzp, HALVES[0], b_xp, l1.at[r, 3]),
            (b_xzm, HALVES[1], b_zm, l1.at[r, 4]),
            (b_xzp, HALVES[1], b_zp, l1.at[r, 5]),
            (b_zm, (0, D), b_zm, l2.at[r, 0]),
            (b_zp, (0, D), b_zp, l2.at[r, 1]),
            (b_xp, (0, D), b_xp, l2.at[r, 2]),
        ]
        return [
            remote(
                p.at[rows(b), pl.ds(*lanes)], land, rs_s.at[r, n], rs_r.at[r, n], {"tensor": to}
            )
            for n, (b, lanes, to, land) in enumerate(plan)
            if lo_n <= n < hi_n
        ]

    def add(r, b, lanes, *landed):
        where = (r, rows(b), pl.ds(*lanes))
        total = pb[where].astype(F32)
        for piece in landed:
            total = total + piece.astype(F32)
        pb[where] = total.astype(BF)

    def rs0(r):
        for c in rs_copies(r, 0, 3):
            c.start()

    def rs1(r):
        for c in rs_copies(r, 0, 3):
            c.wait_recv()
        add(r, b_zz, THIRDS[0], l0[r, :, THIRDS[0][0]:THIRDS[0][0] + THIRDS[0][1]])
        add(r, b_xzm, THIRDS[1], l0[r, :, THIRDS[1][0]:THIRDS[1][0] + THIRDS[1][1]])
        add(r, b_xzp, THIRDS[2], l0[r, :, THIRDS[2][0]:THIRDS[2][0] + THIRDS[2][1]])
        for c in rs_copies(r, 3, 9):
            c.start()

    def rs2(r):
        for c in rs_copies(r, 3, 9):
            c.wait_recv()
        add(r, b_zm, HALVES[0], l1[r, 0], l1[r, 2])
        add(r, b_zp, HALVES[1], l1[r, 1])
        add(r, b_zp, HALVES[0], l1[r, 3])
        add(r, b_xp, HALVES[1], l1[r, 4], l1[r, 5])
        for c in rs_copies(r, 9, 12):
            c.start()

    def normed(x, n):
        inverse = lax.rsqrt(jnp.mean(x * x, axis=-1, keepdims=True) + EPS)
        return (x * inverse * gains_ref[n:n + 1, :]).astype(BF)

    def first(r):
        x = hidden_ref[r]
        res[r] = x
        xg[0, r, rows(b_me), :] = normed(x.astype(F32), 0)

    def rs_sum(r):
        for c in rs_copies(r, 9, 12):
            c.wait_recv()
        total = pb[r, rows(b_me), :].astype(F32)
        for n in range(3):
            total = total + l2[r, n].astype(F32)
        total = (res[r].astype(F32) + total).astype(BF)
        for c in rs_copies(r):
            c.wait_send()
        return total

    def rsf(ph, r):
        total = rs_sum(r)
        res[r] = total
        xg[ph, r, rows(b_me), :] = normed(total.astype(F32), ph)

    def y_copies(buf, base):
        return [
            remote(buf.at[y], buf.at[y], pf_s.at[base], pf_r.at[base], {"req": y_up}),
            remote(buf.at[y], buf.at[y], pf_s.at[base + 1], pf_r.at[base + 1], {"req": y_dn}),
            remote(
                buf.at[lax.rem(y + 3, 4), pl.ds(0, 2)], buf.at[lax.rem(y + 3, 4), pl.ds(0, 2)],
                pf_s.at[base + 2], pf_r.at[base + 2], {"req": y_up},
            ),
            remote(
                buf.at[lax.rem(y + 1, 4), pl.ds(2, 2)], buf.at[lax.rem(y + 1, 4), pl.ds(2, 2)],
                pf_s.at[base + 3], pf_r.at[base + 3], {"req": y_dn},
            ),
        ]

    def y_waits(buf, base):
        far = lax.rem(y + 2, 4)
        got = [
            buf.at[lax.rem(y + 3, 4)],
            buf.at[lax.rem(y + 1, 4)],
            buf.at[far, pl.ds(0, 2)],
            buf.at[far, pl.ds(2, 2)],
        ]
        return [
            remote(ref, ref, pf_s.at[base + n], pf_r.at[base + n], {"req": y_up})
            for n, ref in enumerate(got)
        ]

    def y0(buf, base):
        for c in y_copies(buf, base)[:2]:
            c.start()

    def y1(buf, base):
        for c in y_waits(buf, base)[:2]:
            c.wait_recv()
        for c in y_copies(buf, base)[2:]:
            c.start()

    def yf(buf, base):
        for c in y_waits(buf, base)[2:]:
            c.wait_recv()
        for c in y_copies(buf, base):
            c.wait_send()

    def id_copies():
        return [
            remote(info_ref, idr.at[n], sel_s.at[n], sel_r.at[n], {"req": other})
            for n, other in enumerate(pals)
        ]

    def sel_copies(src, dst, base):
        return [
            remote(src.at[n], dst.at[n], sel_s.at[base + n], sel_r.at[base + n], {"req": other})
            for n, other in enumerate(pals)
        ]

    def pick(buf, sid):
        owner = sid // 4
        mine = jnp.logical_and(owner // 8 == xh, lax.rem(owner, 2) == core)
        flag = jnp.where(mine, 1.0, 0.0).astype(F32)
        return (buf[lax.rem(owner // 2, 4), lax.rem(sid, 4)].astype(F32) * flag).astype(BF)

    def select_send(buf, src, dst, base):
        for n in range(3):
            for r in range(2):
                src[n, r] = pick(buf, ids_smem[n, r, 0])
        for c in sel_copies(src, dst, base):
            c.start()

    def select_fin(buf, src, dst, base, out, size):
        copies = sel_copies(src, dst, base)
        for c in copies:
            c.wait_recv()
        for r in range(2):
            total = pick(buf, ids_ref[r]).astype(F32)
            for n in range(3):
                total = total + dst[n, r].astype(F32)
            out[r, pl.ds(0, size), :] = total.astype(BF)
        for c in copies:
            c.wait_send()

    def build():
        counts = dot_t(fold_ref[...], norms_ref[...].astype(BF)).astype(BF)
        for s in range(4):
            entry = dot(counts, nplace_ref[s]) + dot(tplace_ref[...], tail_ref[s])
            for h in range(2):
                folded = dot(fold_ref[...], sums_ref[s, h].astype(BF)).astype(BF)
                entry = entry + dot(folded, place_ref[h])
            ys[y, s] = entry.astype(BF)

    def prep():
        for c in loads[:4]:
            c.wait()

        @pl.loop(0, 7)
        def _(n):
            part = ds(n * 256, 256)
            wvq[part, :] = jnp.concatenate([vw[part, :], qw[part, :]], axis=1)
            wuk[part, :] = jnp.concatenate([uw[part, :], kw[part, :]], axis=1)

        loads[4].wait()
        lo[pl.ds(224, 32), :] = jnp.zeros((32, D), BF)
        for r in range(2):
            sfin[r, pl.ds(PF, 256 - PF), :] = jnp.zeros((256 - PF, 256), BF)

    def proj(r):
        @pl.loop(0, 2)
        def _(n):
            part = ds(n * 256, 256)
            x = xg[0, r, part, :]
            vqb[r, part, :] = dot(x, wvq[...]).astype(BF)
            ukb[r, part, :] = dot(x, wuk[...]).astype(BF)

    def conv(r):
        vf[pl.ds(0, 16), :] = sfin[r, PF - 16:PF, :].astype(F32)

        @pl.loop(0, 4)
        def _(n):
            part = ds(n * 128, 128)
            vf[pl.ds(pl.multiple_of(n * 128 + 16, 16), 128), :] = vqb[r, part, :].astype(F32)

        lane = lax.broadcasted_iota(jnp.int32, (128, 256), 1)
        for n in range(4):
            s = 16 + n * 128
            c = (
                taps_ref[0:1, :] * vf[s:s + 128, :]
                + taps_ref[1:2, :] * vf[s - 1:s + 127, :]
                + taps_ref[2:3, :] * vf[s - 2:s + 126, :]
            )
            u = ukb[r, n * 128:(n + 1) * 128, :].astype(F32)
            m = c * (u / (1.0 + jnp.exp(-u)))
            m1[r, n * 128:(n + 1) * 128, :] = jnp.where(lane < 224, m, 1.0).astype(BF)

    def attn(r, blocks):
        for n in blocks:
            size = 128 * (n + 1)
            qb = vqb[r, n * 128:size, :]
            lane = lax.broadcasted_iota(jnp.int32, (128, 256), 1)
            row = lax.broadcasted_iota(jnp.int32, (128, size), 0) + n * 128
            col = lax.broadcasted_iota(jnp.int32, (128, size), 1)
            keys = ukb[r, 0:size, :]
            mixed = m1[r, 0:size, :]
            heads = []
            for h in range(2):
                low = 224 + 16 * h
                qh = jnp.where(jnp.logical_and(lane >= low, lane < low + 16), qb.astype(F32), 0.0)
                a = dot_t(qh.astype(BF), keys) * (FD ** (-0.5))
                w = jnp.where(col <= row, 1.0 + a + 0.5 * a * a, 0.0).astype(BF)
                phi = (dot(qb, left_ref[h]) + frow_ref[0:1, :]) * (
                    dot(qb, right_ref[h]) + frow_ref[1:2, :]
                )
                phi = (phi * frow_ref[2:3, :]).astype(BF)
                acc = dot(w, mixed) + dot(phi, sfin[r])
                heads.append(acc / acc[:, 224 + h:225 + h])
            out = jnp.where(lane < HS, heads[0], jnp.where(lane < 2 * HS, heads[1], 0.0))
            pb[r, n * 128:size, :] = dot(out.astype(BF), lo[...]).astype(BF)

    def win_proj(r):
        @pl.loop(0, 2)
        def _(n):
            part = ds(n * 256, 256)
            after = ds(n * 256 + WIN, 256)
            x = xg[1, r, part, :]
            qbuf[r, part, :] = dot(x, wq[...]).astype(BF)
            kbuf[r, after, :] = dot(x, wk[...]).astype(BF)
            vbuf[r, after, :] = dot(x, wv[...]).astype(BF)

        kbuf[r, pl.ds(0, WIN), :] = kvfin[r, 0:64, :]
        vbuf[r, pl.ds(0, WIN), :] = kvfin[r, 64:128, :]

    def win_attn(r, blocks):
        lane = lax.broadcasted_iota(jnp.int32, (128, 224), 1)
        row = lax.broadcasted_iota(jnp.int32, (128, 192), 0)
        col = lax.broadcasted_iota(jnp.int32, (128, 192), 1)
        allowed = jnp.logical_and(col > row, col <= row + WIN)
        position = lax.broadcasted_iota(jnp.int32, (128, 1), 0)
        last = info_ref[2 + r:3 + r, 0:1] - 1
        for n in blocks:
            qb = qbuf[r, n * 128:(n + 1) * 128, :].astype(F32)
            keys = kbuf[r, n * 128:n * 128 + 192, :]
            vals = vbuf[r, n * 128:n * 128 + 192, :]
            heads = []
            best = None
            for h in range(2):
                own = (lane >= HS) if h else (lane < HS)
                e = dot_t(jnp.where(own, qb, 0.0).astype(BF), keys) * (HS ** (-0.5))
                e = jnp.where(allowed, e, -jnp.inf)
                top = jnp.max(e, axis=-1, keepdims=True)
                ex = jnp.exp(e - top)
                p = (ex / jnp.sum(ex, axis=-1, keepdims=True)).astype(BF)
                heads.append(dot(p, vals))
                best = top if best is None else jnp.maximum(best, top)
            hit = jnp.where(position + n * 128 == last, best, -jnp.inf)
            topbuf[r, n:n + 1, :] = jnp.broadcast_to(
                jnp.max(hit, axis=0, keepdims=True), (1, 128)
            )
            out = jnp.where(lane < HS, heads[0], heads[1]).astype(BF)
            pb[r, n * 128:(n + 1) * 128, :] = dot(out, wo[...]).astype(BF)

    def ffn(r, half):
        x = xg[2, r, half * 256:(half + 1) * 256, :]
        for s, e in ((0, 256), (256, 512), (512, 768), (768, 896)):
            g = dot(x, gate[:, s:e])
            u = dot(x, up[:, s:e])
            fbuf[:, s:e] = (g / (1.0 + jnp.exp(-g)) * u).astype(BF)
        f = fbuf[...]
        for s in range(0, D, 256):
            pb[r, half * 256:(half + 1) * 256, s:s + 256] = dot(f, down[:, s:s + 256]).astype(BF)

    def last(r):
        x = rs_sum(r).astype(F32)
        place = lax.broadcasted_iota(jnp.int32, (ROWS, 1), 0) + b_me * ROWS
        x = jnp.where(place < info_ref[2 + r:3 + r, 0:1], x, 0.0)
        out_ref[r] = x.astype(BF)
        total = jnp.sum(jnp.sum(x * x, axis=-1, keepdims=True), axis=0, keepdims=True)
        fins[pl.ds(r, 1), :] = jnp.broadcast_to(total, (1, 128))
        fins[pl.ds(2 + r, 1), :] = jnp.max(topbuf[r], axis=0, keepdims=True)

    first(0)
    topbuf[...] = jnp.full(topbuf.shape, -jnp.inf, F32)
    fins[...] = jnp.zeros(fins.shape, F32)
    pl.semaphore_wait(barrier, 12)
    ag0(0, 0)
    for c in id_copies():
        c.start()
    build()
    y0(ys, 0)
    first(1)
    ag1(0, 0)
    ag0(0, 1)
    for c in kv_loads:
        c.wait()
    prep()
    for n, c in enumerate(id_copies()):
        c.wait()
    to_smem = pltpu.make_async_copy(idr, ids_smem, loc.at[2])
    to_smem.start()
    to_smem.wait()
    y1(ys, 0)
    y0(ykv, 4)
    ag2(0, 0)
    yf(ys, 0)
    select_send(ys, sels, rcvs, 3)
    ag1(0, 1)
    agf(0, 0)
    proj(0)
    y1(ykv, 4)
    ag2(0, 1)
    agf(0, 1)
    proj(1)
    select_fin(ys, sels, rcvs, 3, sfin, PF)
    conv(0)
    attn(0, range(4))
    rs0(0)
    conv(1)
    rs1(0)
    attn(1, range(2))
    yf(ykv, 4)
    select_send(ykv, selkv, rcvkv, 6)
    rs2(0)
    attn(1, range(2, 4))
    rs0(1)
    rsf(1, 0)
    ag0(1, 0)
    rs1(1)
    select_fin(ykv, selkv, rcvkv, 6, kvfin, 128)
    for c in loads[5:9]:
        c.wait()
    ag1(1, 0)
    rs2(1)
    ag2(1, 0)
    rsf(1, 1)
    ag0(1, 1)
    agf(1, 0)
    win_proj(0)
    ag1(1, 1)
    win_attn(0, range(4))
    rs0(0)
    ag2(1, 1)
    for c in loads[9:]:
        c.wait()
    agf(1, 1)
    rs1(0)
    win_proj(1)
    rs2(0)
    win_attn(1, range(4))
    rs0(1)
    rsf(2, 0)
    ag0(2, 0)
    rs1(1)
    ag1(2, 0)
    rs2(1)
    ag2(2, 0)
    rsf(2, 1)
    ag0(2, 1)
    agf(2, 0)
    ffn(0, 0)
    ag1(2, 1)
    ffn(0, 1)
    rs0(0)
    ag2(2, 1)
    agf(2, 1)
    rs1(0)
    ffn(1, 0)
    rs2(0)
    ffn(1, 1)
    rs0(1)
    last(0)
    rs1(1)
    rs2(1)
    last(1)

    ends = [
        remote(fins, fin.at[k - 1], fin_s.at[k - 1], fin_r.at[k - 1], {"tensor": lax.rem(t + k, 8)})
        for k in range(1, 8)
    ]
    for c in ends:
        c.start()
    for c in ends:
        c.wait_recv()
    total = fins[...]
    best = fins[...]
    for k in range(7):
        total = total + fin[k]
        best = jnp.maximum(best, fin[k])
    line = lax.broadcasted_iota(jnp.int32, (8, 128), 0)
    scal_ref[...] = jnp.where(line < 2, jnp.sqrt(total / D), best)
    for c in ends:
        c.wait_send()


def per_device(
    hidden, suffix_len, request_group, group_slot, norm_first, query_weight, key_weight,
    value_weight, filter_gate, filter_taps, linear_out, norm_second, window_query, window_key,
    window_value, window_out, norm_third, gate_weight, up_weight, down_weight, prefix_sums,
    prefix_norms, prefix_keys, prefix_values, prefix_tail,
):
    matches = jnp.arange(group_slot.shape[0])[None, :] == request_group[:, None]
    slot_ids = jnp.sum(jnp.where(matches, group_slot[None, :], 0), axis=1)
    info = jnp.concatenate([slot_ids, suffix_len, jnp.zeros((4,), jnp.int32)])
    info = jnp.broadcast_to(info[:, None], (8, 128))
    gains = jnp.stack([norm_first, norm_second, norm_third])
    taps = jnp.pad(filter_taps, ((0, 5), (0, 32)))
    tail = jnp.pad(prefix_tail, ((0, 0), (0, 6), (0, 32)))
    vm = pl.BlockSpec(memory_space=pltpu.VMEM)
    hbm = pl.BlockSpec(memory_space=pl.ANY)
    vmem = pltpu.VMEM
    dma = pltpu.SemaphoreType.DMA
    scratch = [
        vmem((D, 32), BF), vmem((D, 32), BF), vmem((D, 224), BF), vmem((D, 224), BF),
        vmem((D, 256), BF), vmem((D, 256), BF), vmem((256, D), BF),
        vmem((D, 224), BF), vmem((D, 224), BF), vmem((D, 224), BF), vmem((224, D), BF),
        vmem((D, FFL), BF), vmem((D, FFL), BF), vmem((FFL, D), BF),
        vmem((3, 2, LMAX, D), BF),
        vmem((2, LMAX, D), BF),
        vmem((2, ROWS, D), BF), vmem((2, 6, ROWS, 896), BF), vmem((2, 3, ROWS, D), BF),
        vmem((2, ROWS, D), BF),
        vmem((4, 4, PF, 256), BF), vmem((4, 4, 128, 224), BF),
        vmem((3, 2, PF, 256), BF), vmem((3, 2, 128, 224), BF),
        vmem((3, 2, PF, 256), BF), vmem((3, 2, 128, 224), BF),
        vmem((2, 256, 256), BF), vmem((2, 128, 224), BF),
        vmem((3, 8, 128), jnp.int32), pltpu.SMEM((3, 8, 128), jnp.int32),
        vmem((2, LMAX, 256), BF), vmem((2, LMAX, 256), BF),
        vmem((LMAX + 16, 256), F32), vmem((2, LMAX, 256), BF),
        vmem((16, 256), BF),
        vmem((2, LMAX, 224), BF), vmem((2, LMAX + WIN, 224), BF), vmem((2, LMAX + WIN, 224), BF),
        vmem((256, FFL), BF),
        vmem((2, 8, 128), F32),
        vmem((7, 8, 128), F32), vmem((8, 128), F32),
        dma((12,)),
        dma((2, 12)), dma((2, 12)), dma((2, 12)), dma((2, 12)),
        dma((8,)), dma((8,)), dma((9,)), dma((9,)), dma((7,)), dma((7,)), dma((3,)),
    ]
    out, scal = pl.pallas_call(
        kernel,
        out_shape=(
            jax.ShapeDtypeStruct((2, ROWS, D), BF),
            jax.ShapeDtypeStruct((8, 128), F32),
        ),
        in_specs=[pl.BlockSpec(memory_space=pltpu.SMEM)] + [vm] * 14 + [hbm] * 14,
        out_specs=(vm, vm),
        scratch_shapes=scratch,
        compiler_params=pltpu.CompilerParams(
            collective_id=0, has_side_effects=True, vmem_limit_bytes=67043328
        ),
        name="layer_pair",
    )(
        slot_ids, hidden, gains, taps, info, prefix_sums, prefix_norms.reshape(8, 273), tail,
        *constants(), prefix_keys, prefix_values, query_weight, key_weight, value_weight,
        filter_gate, linear_out, window_query, window_key, window_value, window_out,
        gate_weight, up_weight, down_weight,
    )
    return out, scal[0:2, 0], scal[2:4, 0]


def solution(mesh):
    return jax.shard_map(
        per_device,
        mesh=mesh,
        in_specs=(
            P("req", "tensor", None), P("req"), P("req"), P(), P(),
            P(None, "tensor"), P(None, "tensor"), P(None, "tensor"), P(None, "tensor"),
            P(None, "tensor"), P("tensor", None), P(),
            P(None, "tensor"), P(None, "tensor"), P(None, "tensor"), P("tensor", None), P(),
            P(None, "tensor"), P(None, "tensor"), P("tensor", None),
            P("req", "tensor", None, None), P("req", "tensor", None),
            P("req", None, "tensor"), P("req", None, "tensor"), P("req", None, "tensor"),
        ),
        out_specs=(P("req", "tensor", None), P("req"), P("req")),
        check_vma=False,
    )
```

```python
import jax
import jax.numpy as jnp
import numpy as np
from jax import lax
from jax.experimental import pallas as pl
from jax.experimental.pallas import tpu as pltpu
from jax.sharding import PartitionSpec as P

D = 1792
FD = 16
HS = 112
WIN = 64
LMAX = 512
ROWS = 64
FFL = 896
PF = 160
EPS = 1e-05
BF = jnp.bfloat16
F32 = jnp.float32
MESH = pl.DeviceIdType.MESH
HALVES = ((0, 896), (896, 896))


def constants():
    pairs = [(i, j) for i in range(FD) for j in range(i, FD)]
    fold = np.zeros((PF, 273), np.float32)
    left = np.zeros((2, 256, 256), np.float32)
    right = np.zeros((2, 256, 256), np.float32)
    rows = np.zeros((8, 256), np.float32)
    fold[0, 0] = 1.0
    rows[0, 0] = 1.0
    rows[1, 0] = 1.0
    rows[2, 0] = 1.0
    for i in range(FD):
        fold[1 + i, 1 + i] = 1.0
        for h in range(2):
            left[h, 224 + 16 * h + i, 1 + i] = 1.0
        rows[1, 1 + i] = 1.0
        rows[2, 1 + i] = FD ** (-0.25)
    for n, (i, j) in enumerate(pairs):
        fold[17 + n, 17 + FD * i + j] = 1.0
        fold[17 + n, 17 + FD * j + i] = 1.0
        for h in range(2):
            left[h, 224 + 16 * h + i, 17 + n] = 1.0
            right[h, 224 + 16 * h + j, 17 + n] = 1.0
        rows[2, 17 + n] = (2.0 * FD) ** (-0.5)
    place = np.zeros((3, 112, 256), np.float32)
    for h in range(2):
        for d in range(HS):
            place[h, d, HS * h + d] = 1.0
    norm_place = np.zeros((2, 256), np.float32)
    for h in range(2):
        norm_place[h, 224 + h] = 1.0
    tail_place = np.zeros((PF, 2), np.float32)
    tail_place[158, 0] = 1.0
    tail_place[159, 1] = 1.0
    wide = np.zeros((224, 256), np.float32)
    for d in range(224):
        wide[d, d] = 1.0
    return (
        jnp.asarray(fold, BF),
        jnp.asarray(left, BF),
        jnp.asarray(right, BF),
        jnp.asarray(rows, F32),
        jnp.asarray(place[:2], BF),
        jnp.asarray(norm_place, BF),
        jnp.asarray(tail_place, BF),
        jnp.asarray(wide, BF),
    )


def dot(a, b):
    return jnp.dot(a, b, preferred_element_type=F32)


def dot_t(a, b):
    return lax.dot_general(a, b, (((1,), (1,)), ((), ())), preferred_element_type=F32)

SETS = ((768, D), (896, D), (D, FFL), (D, FFL), (FFL, D))


def kernel(
    group_ref,
    slot_ref,
    len_ref,
    hidden_ref,
    g1_ref,
    g2_ref,
    g3_ref,
    taps_ref,
    sums_ref,
    norms_ref,
    tail_ref,
    fold_ref,
    left_ref,
    right_ref,
    frow_ref,
    place_ref,
    nplace_ref,
    tplace_ref,
    wide_ref,
    keys_hbm,
    values_hbm,
    qw_hbm,
    kw_hbm,
    vw_hbm,
    uw_hbm,
    lo_hbm,
    wq_hbm,
    wk_hbm,
    wv_hbm,
    wo_hbm,
    gate_hbm,
    up_hbm,
    down_hbm,
    out_ref,
    scal_ref,
    lin,
    win,
    gate,
    up,
    down,
    xg,
    pb,
    l0,
    l1,
    res,
    hx,
    ox,
    orx,
    ys,
    ykv,
    sels,
    selkv,
    rcvs,
    rcvkv,
    sfin,
    kvfin,
    info,
    idr,
    ids_smem,
    taps,
    vqb,
    ukb,
    vf,
    m1,
    qbuf,
    kbuf,
    vbuf,
    fbuf,
    topbuf,
    fin,
    fins,
    wsem,
    ag_s,
    ag_r,
    rs_s,
    rs_r,
    pf_s,
    pf_r,
    sel_s,
    sel_r,
    w_s,
    w_r,
    x_s,
    x_r,
    fin_s,
    fin_r,
    loc,
):
    t = lax.axis_index("tensor")
    rq = lax.axis_index("req")
    z = lax.rem(t, 4)
    xl = t // 4
    core = lax.rem(rq, 2)
    y = lax.rem(rq // 2, 4)
    xh = rq // 8
    xx = xh * 2 + xl
    par = lax.rem(y, 2)
    far_c = 1 - xl

    d_zp = {"tensor": xl * 4 + lax.rem(z + 1, 4)}
    d_zm = {"tensor": xl * 4 + lax.rem(z + 3, 4)}
    d_xp = {"tensor": far_c * 4 + z}
    d_yp = {"req": xh * 8 + lax.rem(y + 1, 4) * 2 + core}
    d_ym = {"req": xh * 8 + lax.rem(y + 3, 4) * 2 + core}
    z_p, z_m, z_z = lax.rem(z + 1, 4), lax.rem(z + 3, 4), lax.rem(z + 2, 4)

    def pal(n):
        x2 = lax.rem(xx + n // 2, 4)
        return {
            "req": (x2 // 2) * 8 + y * 2 + lax.rem(core + n % 2, 2),
            "tensor": lax.rem(x2, 2) * 4 + z,
        }

    pals = {n: pal(n) for n in range(1, 8)}

    barrier = pltpu.get_barrier_semaphore()
    for k in range(1, 8):
        pl.semaphore_signal(
            barrier, inc=1, device_id={"tensor": lax.rem(t + k, 8)}, device_id_type=MESH
        )
    for other in [d_yp, d_ym] + list(pals.values()):
        pl.semaphore_signal(barrier, inc=1, device_id=other, device_id_type=MESH)

    local = [
        (vw_hbm, lin.at[0, pl.ds(0, 224)]),
        (qw_hbm, lin.at[0, pl.ds(224, 32)]),
        (uw_hbm, lin.at[0, pl.ds(256, 224)]),
        (kw_hbm, lin.at[0, pl.ds(480, 32)]),
        (lo_hbm, lin.at[0, pl.ds(512, 224)]),
        (wq_hbm, win.at[0, pl.ds(0, 224)]),
        (wk_hbm, win.at[0, pl.ds(224, 224)]),
        (wv_hbm, win.at[0, pl.ds(448, 224)]),
        (wo_hbm, win.at[0, pl.ds(672, 224)]),
        (gate_hbm, gate.at[0]),
        (up_hbm, up.at[0]),
        (down_hbm, down.at[0]),
        (keys_hbm, ykv.at[y, :, pl.ds(0, 64), :]),
        (values_hbm, ykv.at[y, :, pl.ds(64, 64), :]),
    ]
    loads = [pltpu.make_async_copy(src, dst, wsem.at[n]) for n, (src, dst) in enumerate(local)]
    for n in (0, 1, 2, 3, 4, 12, 13, 5, 6, 7, 8, 9, 10, 11):
        loads[n].start()

    def rows(c, b):
        return pl.ds(pl.multiple_of(c * 256 + b * ROWS, ROWS), ROWS)

    def remote(src, dst, ssem, rsem, to):
        return pltpu.make_async_remote_copy(
            src_ref=src, dst_ref=dst, send_sem=ssem, recv_sem=rsem, device_id=to,
            device_id_type=MESH,
        )

    def ag_part(ph, c, n, b, lanes, to):
        ref = xg.at[ph, rows(c, b), pl.ds(*lanes)]
        return remote(ref, ref, ag_s.at[c, n], ag_r.at[c, n], to)

    def ag_sends(ph, c, first_n, end_n):
        plan = (
            (z, HALVES[0], d_zp),
            (z, HALVES[1], d_zm),
            (z, HALVES[1], d_zp),
            (z, HALVES[0], d_zm),
            (z_m, HALVES[0], d_zp),
            (z_p, HALVES[1], d_zm),
        )
        return [ag_part(ph, c, n, *plan[n]) for n in range(first_n, end_n)]

    def ag_waits(ph, c, first_n, end_n):
        got = (
            (z_m, HALVES[0]),
            (z_p, HALVES[1]),
            (z_m, HALVES[1]),
            (z_p, HALVES[0]),
            (z_z, HALVES[0]),
            (z_z, HALVES[1]),
        )
        return [ag_part(ph, c, n, *got[n], d_zp) for n in range(first_n, end_n)]

    def ag0(ph, c):
        for d in ag_sends(ph, c, 0, 4):
            d.start()

    def ag1(ph, c):
        for n in range(2):
            for d in ag_waits(ph, c, n, n + 1):
                d.wait_recv()
            for d in ag_sends(ph, c, n + 4, n + 5):
                d.start()

    def agf(ph, c):
        for d in ag_waits(ph, c, 2, 6):
            d.wait_recv()
        for d in ag_sends(ph, c, 0, 6):
            d.wait_send()

    def rs_parts(c, first_n, end_n):
        plan = (
            (z_z, 0, d_zm, l0.at[c, 0]),
            (z_z, 1, d_zp, l0.at[c, 1]),
            (z_m, 1, d_zm, l1.at[c, 0, 1]),
            (z_p, 0, d_zp, l1.at[c, 1, 0]),
            (z_m, 0, d_zm, l1.at[c, 0, 0]),
            (z_p, 1, d_zp, l1.at[c, 1, 1]),
        )
        out = []
        for n in range(first_n, end_n):
            b, half, to, land = plan[n]
            src = pb.at[rows(c, b), pl.ds(*HALVES[half])]
            out.append(remote(src, land, rs_s.at[c, n], rs_r.at[c, n], to))
        return out

    def rs0(c):
        for d in rs_parts(c, 0, 4):
            d.start()

    def rs1(c):
        for n, b in ((0, z_m), (1, z_p)):
            for d in rs_parts(c, n, n + 1):
                d.wait_recv()
            where = (rows(c, b), pl.ds(*HALVES[n]))
            pb[where] = (pb[where].astype(F32) + l0[c, n].astype(F32)).astype(BF)
            for d in rs_parts(c, n + 4, n + 5):
                d.start()

    def normed(x, g):
        inverse = lax.rsqrt(jnp.mean(x * x, axis=-1, keepdims=True) + EPS)
        return (x * inverse * g[...].reshape(1, D)).astype(BF)

    def rs_sum(c):
        for d in rs_parts(c, 2, 6):
            d.wait_recv()
        parts = []
        for half in range(2):
            where = (rows(c, z), pl.ds(*HALVES[half]))
            total = pb[where].astype(F32) + l1[c, 0, half].astype(F32) + l1[c, 1, half].astype(F32)
            kept = res[c, :, pl.ds(*HALVES[half])].astype(F32)
            parts.append((kept + total).astype(BF))
        for d in rs_parts(c, 0, 6):
            d.wait_send()
        return jnp.concatenate(parts, axis=1)

    def rsf(ph, c, g):
        total = rs_sum(c)
        res[c] = total
        xg[ph, rows(c, z), :] = normed(total.astype(F32), g)
        ag0(ph, c)

    def first(c, x):
        res[c] = x
        xg[0, rows(c, z), :] = normed(x.astype(F32), g1_ref)
        ag0(0, c)

    def swap_in():
        return remote(hidden_ref.at[far_c], hx, x_s.at[0], x_r.at[0], d_xp)

    def swap_out():
        return remote(ox.at[far_c], orx, x_s.at[1], x_r.at[1], d_xp)

    wbufs = (lin, win, gate, up, down)

    def piece(s, which, cc, pp, side, count=1):
        size = SETS[s][0] // 8
        start = (cc * 4 + pp * 2 + side) * size
        return wbufs[s].at[which, pl.ds(pl.multiple_of(start, 16), size * count)]

    def w_copy(s, n, src, dst, to):
        return remote(src, dst, w_s.at[s, n], w_r.at[s, n], to)

    def w_sends(s, n):
        if n == 0:
            return w_copy(s, n, piece(s, 0, core, par, 0), piece(s, 1, core, par, 0), pals[2])
        if n == 1:
            return w_copy(s, n, piece(s, 0, core, par, 1), piece(s, 1, core, par, 1), pals[6])
        if n == 2:
            ref = piece(s, 1, core, par, 0)
            return w_copy(s, n, ref, ref, d_yp)
        if n == 3:
            ref = piece(s, 1, core, par, 1)
            return w_copy(s, n, ref, ref, d_ym)
        ref = piece(s, 1, core, par if n == 4 else 1 - par, 0, 2)
        return w_copy(s, n, ref, ref, pals[1])

    def w_waits(s, n):
        if n < 2:
            ref = piece(s, 1, core, par, n)
        elif n < 4:
            ref = piece(s, 1, core, 1 - par, n - 2)
        else:
            ref = piece(s, 1, 1 - core, par if n == 4 else 1 - par, 0, 2)
        return w_copy(s, n, ref, ref, pals[1])

    def w0(s):
        for n in range(2):
            w_sends(s, n).start()

    def w1(s):
        for n in range(2):
            w_waits(s, n).wait_recv()
            w_sends(s, n + 2).start()
        w_sends(s, 4).start()

    def w2(s):
        for n in range(2, 4):
            w_waits(s, n).wait_recv()
        w_sends(s, 5).start()

    def wf(s):
        for n in range(4, 6):
            w_waits(s, n).wait_recv()
        for n in range(6):
            w_sends(s, n).wait_send()

    def y_sends(buf, base, n):
        owner = (y, y, y, y, lax.rem(y + 3, 4), lax.rem(y + 1, 4))[n]
        ref = buf.at[owner, pl.ds((0, 2, 2, 0, 0, 2)[n], 2)]
        return remote(ref, ref, pf_s.at[base + n], pf_r.at[base + n], d_ym if n % 2 else d_yp)

    def y_waits(buf, base, n):
        before, after, across = lax.rem(y + 3, 4), lax.rem(y + 1, 4), lax.rem(y + 2, 4)
        owner = (before, after, before, after, across, across)[n]
        ref = buf.at[owner, pl.ds((0, 2, 2, 0, 0, 2)[n], 2)]
        return remote(ref, ref, pf_s.at[base + n], pf_r.at[base + n], d_yp)

    def y0(buf, base):
        for n in range(4):
            y_sends(buf, base, n).start()

    def y1(buf, base):
        for n in range(2):
            y_waits(buf, base, n).wait_recv()
            y_sends(buf, base, n + 4).start()

    def yf(buf, base):
        for n in range(2, 6):
            y_waits(buf, base, n).wait_recv()
        for n in range(6):
            y_sends(buf, base, n).wait_send()

    def id_copy(n):
        return remote(info, idr.at[n], sel_s.at[n], sel_r.at[n], pals[n])

    def sel_copy(src, dst, base, n):
        return remote(src.at[n], dst.at[n], sel_s.at[base + n], sel_r.at[base + n], pals[n])

    def back(n):
        return ((4 - n // 2) % 4) * 2 + n % 2

    def pick(buf, sid):
        owner = sid // 4
        mine = jnp.logical_and(owner // 8 == xh, lax.rem(owner, 2) == core)
        flag = jnp.where(mine, 1.0, 0.0).astype(F32)
        return buf[lax.rem(owner // 2, 4), lax.rem(sid, 4)].astype(F32) * flag

    def select_send(buf, src, dst, base):
        for n in (4, 5, 2, 3, 6, 7, 1):
            src[n] = pick(buf, ids_smem[back(n), 0, 0]).astype(BF)
            sel_copy(src, dst, base, n).start()

    def select_fin(buf, src, dst, base, out, size):
        for n in range(1, 8):
            sel_copy(src, dst, base, n).wait_recv()
        total = pick(buf, my_slot)
        for n in (1, 4, 5):
            total = total + dst[n].astype(F32)
        out[0, pl.ds(0, size), :] = total.astype(BF)
        total = dst[2].astype(F32)
        for n in (3, 6, 7):
            total = total + dst[n].astype(F32)
        out[1, pl.ds(0, size), :] = total.astype(BF)
        for n in range(1, 8):
            sel_copy(src, dst, base, n).wait_send()

    def build():
        for s in range(4):
            counts = dot_t(fold_ref[...], norms_ref[s].astype(BF)).astype(BF)
            tail = dot(tplace_ref[...], tail_ref[s]).astype(BF)
            entry = dot(counts, nplace_ref[...]) + dot(tail, wide_ref[...])
            for h in range(2):
                folded = dot(fold_ref[...], sums_ref[s, h].astype(BF)).astype(BF)
                entry = entry + dot(folded, place_ref[h])
            ys[y, s] = entry.astype(BF)

    def proj(sh):
        @pl.loop(0, 2)
        def _(c):
            part = pl.ds(pl.multiple_of(c * 256, 256), 256)
            x = xg[0, part, :]
            vqb[sh, part, :] = dot_t(x, lin[sh, 0:256, :]).astype(BF)
            ukb[sh, part, :] = dot_t(x, lin[sh, 256:512, :]).astype(BF)

    def conv(sh):
        vf[pl.ds(0, 16), :] = sfin[sh, PF - 16:PF, :].astype(F32)
        vf[pl.ds(16, LMAX), :] = vqb[sh].astype(F32)
        lane = lax.broadcasted_iota(jnp.int32, (128, 256), 1)
        for n in range(4):
            s = 16 + n * 128
            c = (
                taps[sh, 0:1, :] * vf[s:s + 128, :]
                + taps[sh, 1:2, :] * vf[s - 1:s + 127, :]
                + taps[sh, 2:3, :] * vf[s - 2:s + 126, :]
            )
            u = ukb[sh, n * 128:(n + 1) * 128, :].astype(F32)
            m = c * (u / (1.0 + jnp.exp(-u)))
            m1[sh, n * 128:(n + 1) * 128, :] = jnp.where(lane < 224, m, 1.0).astype(BF)

    def attn(blocks):
        for n in blocks:
            size = 128 * (n + 1)
            lane = lax.broadcasted_iota(jnp.int32, (128, 256), 1)
            row = lax.broadcasted_iota(jnp.int32, (128, size), 0) + n * 128
            col = lax.broadcasted_iota(jnp.int32, (128, size), 1)
            partial = None
            for sh in range(2):
                qb = vqb[sh, n * 128:size, :]
                keys = ukb[sh, 0:size, :]
                mixed = m1[sh, 0:size, :]
                heads = []
                for h in range(2):
                    low = 224 + 16 * h
                    own = jnp.logical_and(lane >= low, lane < low + 16)
                    qh = jnp.where(own, qb.astype(F32), 0.0).astype(BF)
                    a = dot_t(qh, keys) * (FD ** (-0.5))
                    w = jnp.where(col <= row, 1.0 + a + 0.5 * a * a, 0.0).astype(BF)
                    phi = (dot(qb, left_ref[h]) + frow_ref[0:1, :]) * (
                        dot(qb, right_ref[h]) + frow_ref[1:2, :]
                    )
                    phi = (phi * frow_ref[2:3, :]).astype(BF)
                    acc = dot(w, mixed) + dot(phi, sfin[sh])
                    heads.append(acc / acc[:, 224 + h:225 + h])
                out = jnp.where(lane < HS, heads[0], jnp.where(lane < 2 * HS, heads[1], 0.0))
                term = dot(out.astype(BF), lin[sh, 512:768, :])
                partial = term if partial is None else partial + term
            pb[n * 128:size, :] = partial.astype(BF)

    def win_proj(c):
        part = slice(c * 256, c * 256 + 256)
        after = slice(c * 256 + WIN, c * 256 + WIN + 256)

        @pl.loop(0, 2)
        def _(sh):
            x = xg[1, part, :]
            qbuf[sh, part, :] = dot_t(x, win[sh, 0:224, :]).astype(BF)
            kbuf[sh, after, :] = dot_t(x, win[sh, 224:448, :]).astype(BF)
            vbuf[sh, after, :] = dot_t(x, win[sh, 448:672, :]).astype(BF)

    def win_prefix():
        for sh in range(2):
            kbuf[sh, pl.ds(0, WIN), :] = kvfin[sh, 0:64, :]
            vbuf[sh, pl.ds(0, WIN), :] = kvfin[sh, 64:128, :]

    def win_attn(blocks):
        lane = lax.broadcasted_iota(jnp.int32, (128, 224), 1)
        row = lax.broadcasted_iota(jnp.int32, (128, 192), 0)
        col = lax.broadcasted_iota(jnp.int32, (128, 192), 1)
        allowed = jnp.logical_and(col > row, col <= row + WIN)
        position = lax.broadcasted_iota(jnp.int32, (128, 1), 0)
        for n in blocks:
            best = None
            partial = None
            for sh in range(2):
                qb = qbuf[sh, n * 128:(n + 1) * 128, :].astype(F32)
                keys = kbuf[sh, n * 128:n * 128 + 192, :]
                vals = vbuf[sh, n * 128:n * 128 + 192, :]
                heads = []
                for h in range(2):
                    own = (lane >= HS) if h else (lane < HS)
                    e = dot_t(jnp.where(own, qb, 0.0).astype(BF), keys) * (HS ** (-0.5))
                    e = jnp.where(allowed, e, -jnp.inf)
                    top = jnp.max(e, axis=-1, keepdims=True)
                    ex = jnp.exp(e - top)
                    p = (ex / jnp.sum(ex, axis=-1, keepdims=True)).astype(BF)
                    heads.append(dot(p, vals))
                    best = top if best is None else jnp.maximum(best, top)
                out = jnp.where(lane < HS, heads[0], heads[1]).astype(BF)
                term = dot(out, win[sh, 672:896, :])
                partial = term if partial is None else partial + term
            hit = jnp.where(position + n * 128 == length - 1, best, -jnp.inf)
            topbuf[n:n + 1, :] = jnp.broadcast_to(jnp.max(hit, axis=0, keepdims=True), (1, 128))
            pb[n * 128:(n + 1) * 128, :] = partial.astype(BF)

    def ffn_in(c):
        @pl.loop(0, 2)
        def _(sh):
            x = xg[2, c * 256:(c + 1) * 256, :]
            for s, e in ((0, 256), (256, 512), (512, 768), (768, 896)):
                g = dot(x, gate[sh, :, s:e])
                u = dot(x, up[sh, :, s:e])
                fbuf[sh, :, s:e] = (g / (1.0 + jnp.exp(-g)) * u).astype(BF)

    def ffn_out(c):
        for s in range(0, D, 256):
            total = dot(fbuf[0], down[0, :, s:s + 256]) + dot(fbuf[1], down[1, :, s:s + 256])
            pb[c * 256:(c + 1) * 256, s:s + 256] = total.astype(BF)

    def last(c):
        x = rs_sum(c).astype(F32)
        place = lax.broadcasted_iota(jnp.int32, (ROWS, 1), 0) + c * 256 + z * ROWS
        x = jnp.where(place < length, x, 0.0)
        ox[c] = x.astype(BF)
        return jnp.sum(jnp.sum(x * x, axis=-1, keepdims=True), axis=0, keepdims=True)

    my_slot = slot_ref[group_ref[xl]]
    length = len_ref[xl]
    info[...] = jnp.full((8, 128), my_slot, jnp.int32)
    build()
    pl.semaphore_wait(barrier, 16)
    y0(ys, 0)
    swap_in().start()
    for n in range(1, 8):
        id_copy(n).start()
    first(xl, hidden_ref[xl])
    lin[0, pl.ds(736, 32), :] = jnp.zeros((32, D), BF)
    for n in range(5):
        loads[n].wait()
    w0(0)
    taps[0] = jnp.zeros((8, 256), F32)
    taps[0, 0:3, 0:224] = taps_ref[...]
    for sh in range(2):
        sfin[sh, pl.ds(PF, 256 - PF), :] = jnp.zeros((256 - PF, 256), BF)
    topbuf[...] = jnp.full(topbuf.shape, -jnp.inf, F32)
    tap_swap = remote(taps.at[0], taps.at[1], x_s.at[2], x_r.at[2], d_xp)
    tap_swap.start()
    swap_in().wait_recv()
    first(far_c, hx[...])
    y1(ys, 0)
    for n in range(1, 8):
        id_copy(n).wait_recv()
    to_smem = pltpu.make_async_copy(idr, ids_smem, loc.at[0])
    to_smem.start()
    to_smem.wait()
    ag1(0, xl)
    ag1(0, far_c)
    w1(0)
    yf(ys, 0)
    select_send(ys, sels, rcvs, 8)
    loads[12].wait()
    loads[13].wait()
    y0(ykv, 6)
    agf(0, 0)
    agf(0, 1)
    proj(0)
    for n in range(5, 9):
        loads[n].wait()
    w0(1)
    w2(0)
    y1(ykv, 6)
    wf(0)
    proj(1)
    tap_swap.wait()
    select_fin(ys, sels, rcvs, 8, sfin, PF)
    conv(0)
    conv(1)
    attn((0, 1))
    rs0(0)
    w1(1)
    yf(ykv, 6)
    select_send(ykv, selkv, rcvkv, 16)
    for n in range(9, 12):
        loads[n].wait()
    w0(2)
    w0(3)
    w0(4)
    attn((2,))
    rs1(0)
    attn((3,))
    rs0(1)
    w2(1)
    rsf(1, 0, g2_ref)
    rs1(1)
    select_fin(ykv, selkv, rcvkv, 16, kvfin, 128)
    win_prefix()
    wf(1)
    ag1(1, 0)
    rsf(1, 1, g2_ref)
    w1(2)
    agf(1, 0)
    win_proj(0)
    ag1(1, 1)
    win_attn((0, 1))
    rs0(0)
    w1(3)
    w2(2)
    agf(1, 1)
    win_proj(1)
    rs1(0)
    win_attn((2, 3))
    rs0(1)
    rsf(2, 0, g3_ref)
    w1(4)
    w2(3)
    rs1(1)
    ag1(2, 0)
    w2(4)
    rsf(2, 1, g3_ref)
    agf(2, 0)
    for n in (2, 3, 4):
        wf(n)
    ffn_in(0)
    ag1(2, 1)
    ffn_out(0)
    rs0(0)
    agf(2, 1)
    rs1(0)
    ffn_in(1)
    ffn_out(1)
    rs0(1)
    squares = last(0)
    rs1(1)
    squares = squares + last(1)
    swap_out().start()
    line = lax.broadcasted_iota(jnp.int32, (8, 128), 0)
    top = jnp.max(topbuf[...], axis=0, keepdims=True)
    fins[...] = jnp.where(
        line == xl, squares, jnp.where(line == 2 + xl, top, jnp.where(line < 2, 0.0, -jnp.inf))
    )
    ends = [
        remote(fins, fin.at[k - 1], fin_s.at[k - 1], fin_r.at[k - 1], {"tensor": lax.rem(t + k, 8)})
        for k in range(1, 8)
    ]
    for d in ends:
        d.start()
    out_ref[xl] = ox[xl]
    for d in ends:
        d.wait_recv()
    total = fins[...]
    best = fins[...]
    for k in range(7):
        total = total + fin[k]
        best = jnp.maximum(best, fin[k])
    scal_ref[...] = jnp.where(line < 2, jnp.sqrt(total / D), best)
    swap_out().wait_recv()
    out_ref[far_c] = orx[...]
    swap_out().wait_send()
    swap_in().wait_send()
    for n in range(1, 8):
        id_copy(n).wait_send()
    for d in ends:
        d.wait_send()


def per_device(
    hidden, suffix_len, request_group, group_slot, norm_first, query_weight, key_weight,
    value_weight, filter_gate, filter_taps, linear_out, norm_second, window_query, window_key,
    window_value, window_out, norm_third, gate_weight, up_weight, down_weight, prefix_sums,
    prefix_norms, prefix_keys, prefix_values, prefix_tail,
):
    vm = pl.BlockSpec(memory_space=pltpu.VMEM)
    hbm = pl.BlockSpec(memory_space=pl.ANY)
    smem = pl.BlockSpec(memory_space=pltpu.SMEM)
    vmem = pltpu.VMEM
    dma = pltpu.SemaphoreType.DMA
    scratch = [vmem((2,) + shape, BF) for shape in SETS] + [
        vmem((3, LMAX, D), BF),
        vmem((LMAX, D), BF),
        vmem((2, 2, ROWS, 896), BF), vmem((2, 2, 2, ROWS, 896), BF),
        vmem((2, ROWS, D), BF), vmem((ROWS, D), BF), vmem((2, ROWS, D), BF), vmem((ROWS, D), BF),
        vmem((4, 4, PF, 256), BF), vmem((4, 4, 128, 224), BF),
        vmem((8, PF, 256), BF), vmem((8, 128, 224), BF),
        vmem((8, PF, 256), BF), vmem((8, 128, 224), BF),
        vmem((2, 256, 256), BF), vmem((2, 128, 224), BF),
        vmem((8, 128), jnp.int32), vmem((8, 8, 128), jnp.int32),
        pltpu.SMEM((8, 8, 128), jnp.int32),
        vmem((2, 8, 256), F32),
        vmem((2, LMAX, 256), BF), vmem((2, LMAX, 256), BF),
        vmem((LMAX + 16, 256), F32), vmem((2, LMAX, 256), BF),
        vmem((2, LMAX, 224), BF), vmem((2, LMAX + WIN, 224), BF), vmem((2, LMAX + WIN, 224), BF),
        vmem((2, 256, FFL), BF),
        vmem((8, 128), F32),
        vmem((7, 8, 128), F32), vmem((8, 128), F32),
        dma((14,)),
        dma((2, 6)), dma((2, 6)), dma((2, 6)), dma((2, 6)),
        dma((12,)), dma((12,)), dma((24,)), dma((24,)),
        dma((5, 6)), dma((5, 6)), dma((3,)), dma((3,)), dma((7,)), dma((7,)), dma((1,)),
    ]
    out, scal = pl.pallas_call(
        kernel,
        out_shape=(
            jax.ShapeDtypeStruct((2, ROWS, D), BF),
            jax.ShapeDtypeStruct((8, 128), F32),
        ),
        in_specs=[smem] * 3 + [vm] * 16 + [hbm] * 14,
        out_specs=(vm, vm),
        scratch_shapes=scratch,
        compiler_params=pltpu.CompilerParams(
            collective_id=0, has_side_effects=True, vmem_limit_bytes=67043328
        ),
        name="layer_pair",
    )(
        request_group, group_slot, suffix_len, hidden, norm_first, norm_second, norm_third,
        filter_taps, prefix_sums, prefix_norms, prefix_tail, *constants(),
        prefix_keys, prefix_values, query_weight.T, key_weight.T, value_weight.T,
        filter_gate.T, linear_out, window_query.T, window_key.T, window_value.T, window_out,
        gate_weight, up_weight, down_weight,
    )
    return out, scal[0:2, 0], scal[2:4, 0]


def solution(mesh):
    return jax.shard_map(
        per_device,
        mesh=mesh,
        in_specs=(
            P("req", "tensor", None), P("req"), P("req"), P(), P(),
            P(None, "tensor"), P(None, "tensor"), P(None, "tensor"), P(None, "tensor"),
            P(None, "tensor"), P("tensor", None), P(),
            P(None, "tensor"), P(None, "tensor"), P(None, "tensor"), P("tensor", None), P(),
            P(None, "tensor"), P(None, "tensor"), P("tensor", None),
            P("req", "tensor", None, None), P("req", "tensor", None),
            P("req", None, "tensor"), P("req", None, "tensor"), P("req", None, "tensor"),
        ),
        out_specs=(P("req", "tensor", None), P("req"), P("req")),
        check_vma=False,
    )
```

```python
import jax
import jax.numpy as jnp
import numpy as np
from jax import lax
from jax.experimental import pallas as pl
from jax.experimental.pallas import tpu as pltpu
from jax.sharding import PartitionSpec as P

D = 1792
FD = 16
HS = 112
WIN = 64
LMAX = 512
ROWS = 64
FFL = 896
PF = 160
EPS = 1e-05
BF = jnp.bfloat16
F32 = jnp.float32
MESH = pl.DeviceIdType.MESH
HALVES = ((0, 896), (896, 896))


def constants():
    pairs = [(i, j) for i in range(FD) for j in range(i, FD)]
    fold = np.zeros((PF, 273), np.float32)
    left = np.zeros((2, 256, 256), np.float32)
    right = np.zeros((2, 256, 256), np.float32)
    rows = np.zeros((8, 256), np.float32)
    fold[0, 0] = 1.0
    rows[0, 0] = 1.0
    rows[1, 0] = 1.0
    rows[2, 0] = 1.0
    for i in range(FD):
        fold[1 + i, 1 + i] = 1.0
        for h in range(2):
            left[h, 224 + 16 * h + i, 1 + i] = 1.0
        rows[1, 1 + i] = 1.0
        rows[2, 1 + i] = FD ** (-0.25)
    for n, (i, j) in enumerate(pairs):
        fold[17 + n, 17 + FD * i + j] = 1.0
        fold[17 + n, 17 + FD * j + i] = 1.0
        for h in range(2):
            left[h, 224 + 16 * h + i, 17 + n] = 1.0
            right[h, 224 + 16 * h + j, 17 + n] = 1.0
        rows[2, 17 + n] = (2.0 * FD) ** (-0.5)
    norm_place = np.zeros((2, 256), np.float32)
    for h in range(2):
        norm_place[h, 224 + h] = 1.0
    tail_place = np.zeros((PF, 2), np.float32)
    tail_place[158, 0] = 1.0
    tail_place[159, 1] = 1.0
    fold_slots = np.zeros((2 * PF, 546), np.float32)
    for h in range(2):
        fold_slots[h * PF:(h + 1) * PF, h::2] = fold
    return (
        jnp.asarray(fold, BF),
        jnp.asarray(fold_slots, BF),
        jnp.asarray(left, BF),
        jnp.asarray(right, BF),
        jnp.asarray(rows, F32),
        jnp.asarray(norm_place, BF),
        jnp.asarray(tail_place, BF),
    )


def dot(a, b):
    return jnp.dot(a, b, preferred_element_type=F32)


def dot_t(a, b):
    return lax.dot_general(a, b, (((1,), (1,)), ((), ())), preferred_element_type=F32)

SETS = ((512, D), (896, D), (D, FFL), (D, FFL), (FFL, D), (256, D))


def kernel(
    group_ref,
    slot_ref,
    len_ref,
    hidden_ref,
    g1_ref,
    g2_ref,
    g3_ref,
    taps_ref,
    sums_ref,
    norms_ref,
    tail_ref,
    fold_ref,
    fslot_ref,
    left_ref,
    right_ref,
    frow_ref,
    nplace_ref,
    tplace_ref,
    keys_hbm,
    values_hbm,
    qw_hbm,
    kw_hbm,
    vw_hbm,
    uw_hbm,
    lo_hbm,
    wq_hbm,
    wk_hbm,
    wv_hbm,
    wo_hbm,
    gate_hbm,
    up_hbm,
    down_hbm,
    out_ref,
    scal_ref,
    lin,
    win,
    gate,
    up,
    down,
    lows,
    xg,
    pb,
    l0,
    l1,
    res,
    hx,
    ox,
    orx,
    ys,
    ykv,
    sels,
    selkv,
    rcvs,
    rcvkv,
    sfin,
    kvfin,
    info,
    idr,
    ids_smem,
    taps,
    vqb,
    ukb,
    vf,
    m1,
    qbuf,
    kbuf,
    vbuf,
    fbuf,
    topbuf,
    fin,
    fins,
    wsem,
    ag_s,
    ag_r,
    rs_s,
    rs_r,
    pf_s,
    pf_r,
    sel_s,
    sel_r,
    w_s,
    w_r,
    x_s,
    x_r,
    fin_s,
    fin_r,
    loc,
):
    t = lax.axis_index("tensor")
    rq = lax.axis_index("req")
    z = lax.rem(t, 4)
    xl = t // 4
    core = lax.rem(rq, 2)
    y = lax.rem(rq // 2, 4)
    xh = rq // 8
    xx = xh * 2 + xl
    par = lax.rem(y, 2)
    far_c = 1 - xl

    d_zp = {"tensor": xl * 4 + lax.rem(z + 1, 4)}
    d_zm = {"tensor": xl * 4 + lax.rem(z + 3, 4)}
    d_xp = {"tensor": far_c * 4 + z}
    d_yp = {"req": xh * 8 + lax.rem(y + 1, 4) * 2 + core}
    d_ym = {"req": xh * 8 + lax.rem(y + 3, 4) * 2 + core}
    z_p, z_m, z_z = lax.rem(z + 1, 4), lax.rem(z + 3, 4), lax.rem(z + 2, 4)

    def pal(n):
        x2 = lax.rem(xx + n // 2, 4)
        return {
            "req": (x2 // 2) * 8 + y * 2 + lax.rem(core + n % 2, 2),
            "tensor": lax.rem(x2, 2) * 4 + z,
        }

    pals = {n: pal(n) for n in range(1, 8)}

    barrier = pltpu.get_barrier_semaphore()
    for k in range(1, 8):
        pl.semaphore_signal(
            barrier, inc=1, device_id={"tensor": lax.rem(t + k, 8)}, device_id_type=MESH
        )
    for other in [d_yp, d_ym] + list(pals.values()):
        pl.semaphore_signal(barrier, inc=1, device_id=other, device_id_type=MESH)

    local = [
        (vw_hbm, lin.at[0, pl.ds(0, 224)]),
        (qw_hbm, lin.at[0, pl.ds(224, 32)]),
        (uw_hbm, lin.at[0, pl.ds(256, 224)]),
        (kw_hbm, lin.at[0, pl.ds(480, 32)]),
        (lo_hbm, lows.at[0, pl.ds(0, 224)]),
        (wq_hbm, win.at[0, pl.ds(0, 224)]),
        (wk_hbm, win.at[0, pl.ds(224, 224)]),
        (wv_hbm, win.at[0, pl.ds(448, 224)]),
        (wo_hbm, win.at[0, pl.ds(672, 224)]),
        (gate_hbm, gate.at[0]),
        (up_hbm, up.at[0]),
        (down_hbm, down.at[0]),
        (keys_hbm, ykv.at[y, :, pl.ds(0, 64), :]),
        (values_hbm, ykv.at[y, :, pl.ds(64, 64), :]),
    ]
    loads = [pltpu.make_async_copy(src, dst, wsem.at[n]) for n, (src, dst) in enumerate(local)]
    for n in (0, 1, 2, 3, 4, 12, 13, 5, 6, 7, 8, 9, 10, 11):
        loads[n].start()

    def rows(c, b):
        return pl.ds(pl.multiple_of(c * 256 + b * ROWS, ROWS), ROWS)

    def remote(src, dst, ssem, rsem, to):
        return pltpu.make_async_remote_copy(
            src_ref=src, dst_ref=dst, send_sem=ssem, recv_sem=rsem, device_id=to,
            device_id_type=MESH,
        )

    def ag_part(ph, c, n, b, lanes, to):
        ref = xg.at[ph, rows(c, b), pl.ds(*lanes)]
        return remote(ref, ref, ag_s.at[c, n], ag_r.at[c, n], to)

    def ag_sends(ph, c, first_n, end_n):
        plan = (
            (z, HALVES[0], d_zp),
            (z, HALVES[1], d_zm),
            (z, HALVES[1], d_zp),
            (z, HALVES[0], d_zm),
            (z_m, HALVES[0], d_zp),
            (z_p, HALVES[1], d_zm),
        )
        return [ag_part(ph, c, n, *plan[n]) for n in range(first_n, end_n)]

    def ag_waits(ph, c, first_n, end_n):
        got = (
            (z_m, HALVES[0]),
            (z_p, HALVES[1]),
            (z_m, HALVES[1]),
            (z_p, HALVES[0]),
            (z_z, HALVES[0]),
            (z_z, HALVES[1]),
        )
        return [ag_part(ph, c, n, *got[n], d_zp) for n in range(first_n, end_n)]

    def ag0(ph, c):
        for d in ag_sends(ph, c, 0, 4):
            d.start()

    def ag1(ph, c):
        for n in range(2):
            for d in ag_waits(ph, c, n, n + 1):
                d.wait_recv()
            for d in ag_sends(ph, c, n + 4, n + 5):
                d.start()

    def agf(ph, c):
        for d in ag_waits(ph, c, 2, 6):
            d.wait_recv()
        for d in ag_sends(ph, c, 0, 6):
            d.wait_send()

    def rs_parts(c, first_n, end_n):
        plan = (
            (z_z, 0, d_zm, l0.at[c, 0]),
            (z_z, 1, d_zp, l0.at[c, 1]),
            (z_m, 1, d_zm, l1.at[c, 0, 1]),
            (z_p, 0, d_zp, l1.at[c, 1, 0]),
            (z_m, 0, d_zm, l1.at[c, 0, 0]),
            (z_p, 1, d_zp, l1.at[c, 1, 1]),
        )
        out = []
        for n in range(first_n, end_n):
            b, half, to, land = plan[n]
            src = pb.at[rows(c, b), pl.ds(*HALVES[half])]
            out.append(remote(src, land, rs_s.at[c, n], rs_r.at[c, n], to))
        return out

    def rs0(c):
        for d in rs_parts(c, 0, 4):
            d.start()

    def rs1(c):
        for n, b in ((0, z_m), (1, z_p)):
            for d in rs_parts(c, n, n + 1):
                d.wait_recv()
            where = (rows(c, b), pl.ds(*HALVES[n]))
            pb[where] = (pb[where].astype(F32) + l0[c, n].astype(F32)).astype(BF)
            for d in rs_parts(c, n + 4, n + 5):
                d.start()

    def normed(x, g):
        inverse = lax.rsqrt(jnp.mean(x * x, axis=-1, keepdims=True) + EPS)
        return (x * inverse * g[...].reshape(1, D)).astype(BF)

    def rs_sum(c):
        for d in rs_parts(c, 2, 6):
            d.wait_recv()
        parts = []
        for half in range(2):
            where = (rows(c, z), pl.ds(*HALVES[half]))
            total = pb[where].astype(F32) + l1[c, 0, half].astype(F32) + l1[c, 1, half].astype(F32)
            kept = res[c, :, pl.ds(*HALVES[half])].astype(F32)
            parts.append((kept + total).astype(BF))
        for d in rs_parts(c, 0, 6):
            d.wait_send()
        return jnp.concatenate(parts, axis=1)

    def rsf(ph, c, g):
        total = rs_sum(c)
        res[c] = total
        xg[ph, rows(c, z), :] = normed(total.astype(F32), g)
        ag0(ph, c)

    def first(c, x):
        res[c] = x
        xg[0, rows(c, z), :] = normed(x.astype(F32), g1_ref)
        ag0(0, c)

    def swap_in():
        return remote(hidden_ref.at[far_c], hx, x_s.at[0], x_r.at[0], d_xp)

    def swap_out():
        return remote(ox.at[far_c], orx, x_s.at[1], x_r.at[1], d_xp)

    wbufs = (lin, win, gate, up, down, lows)

    def piece(s, which, cc, pp, side, count=1):
        size = SETS[s][0] // 8
        start = (cc * 4 + pp * 2 + side) * size
        return wbufs[s].at[which, pl.ds(pl.multiple_of(start, 16), size * count)]

    def w_copy(s, n, src, dst, to):
        return remote(src, dst, w_s.at[s, n], w_r.at[s, n], to)

    def w_sends(s, n):
        if n == 0:
            return w_copy(s, n, piece(s, 0, core, par, 0), piece(s, 1, core, par, 0), pals[2])
        if n == 1:
            return w_copy(s, n, piece(s, 0, core, par, 1), piece(s, 1, core, par, 1), pals[6])
        if n == 2:
            ref = piece(s, 1, core, par, 0)
            return w_copy(s, n, ref, ref, d_yp)
        if n == 3:
            ref = piece(s, 1, core, par, 1)
            return w_copy(s, n, ref, ref, d_ym)
        ref = piece(s, 1, core, par if n == 4 else 1 - par, 0, 2)
        return w_copy(s, n, ref, ref, pals[1])

    def w_waits(s, n):
        if n < 2:
            ref = piece(s, 1, core, par, n)
        elif n < 4:
            ref = piece(s, 1, core, 1 - par, n - 2)
        else:
            ref = piece(s, 1, 1 - core, par if n == 4 else 1 - par, 0, 2)
        return w_copy(s, n, ref, ref, pals[1])

    def w0(s):
        for n in range(2):
            w_sends(s, n).start()

    def w1(s):
        for n in range(2):
            w_waits(s, n).wait_recv()
            w_sends(s, n + 2).start()
        w_sends(s, 4).start()

    def w2(s):
        for n in range(2, 4):
            w_waits(s, n).wait_recv()
        w_sends(s, 5).start()

    def wf(s):
        for n in range(4, 6):
            w_waits(s, n).wait_recv()
        for n in range(6):
            w_sends(s, n).wait_send()

    def y_sends(buf, base, n):
        owner = (y, y, y, y, lax.rem(y + 3, 4), lax.rem(y + 1, 4))[n]
        ref = buf.at[owner, pl.ds((0, 2, 2, 0, 0, 2)[n], 2)]
        return remote(ref, ref, pf_s.at[base + n], pf_r.at[base + n], d_ym if n % 2 else d_yp)

    def y_waits(buf, base, n):
        before, after, across = lax.rem(y + 3, 4), lax.rem(y + 1, 4), lax.rem(y + 2, 4)
        owner = (before, after, before, after, across, across)[n]
        ref = buf.at[owner, pl.ds((0, 2, 2, 0, 0, 2)[n], 2)]
        return remote(ref, ref, pf_s.at[base + n], pf_r.at[base + n], d_yp)

    def y0(buf, base):
        for n in range(4):
            y_sends(buf, base, n).start()

    def y1(buf, base):
        for n in range(2):
            y_waits(buf, base, n).wait_recv()
            y_sends(buf, base, n + 4).start()

    def yf(buf, base):
        for n in range(2, 6):
            y_waits(buf, base, n).wait_recv()
        for n in range(6):
            y_sends(buf, base, n).wait_send()

    def id_copy(n):
        return remote(info, idr.at[n], sel_s.at[n], sel_r.at[n], pals[n])

    def sel_copy(src, dst, base, n):
        return remote(src.at[n], dst.at[n], sel_s.at[base + n], sel_r.at[base + n], pals[n])

    def back(n):
        return ((4 - n // 2) % 4) * 2 + n % 2

    def pick(buf, sid):
        owner = sid // 4
        mine = jnp.logical_and(owner // 8 == xh, lax.rem(owner, 2) == core)
        flag = jnp.where(mine, 1.0, 0.0).astype(F32)
        return buf[lax.rem(owner // 2, 4), lax.rem(sid, 4)].astype(F32) * flag

    def select_send(buf, src, dst, base):
        for n in (4, 5, 2, 3, 6, 7, 1):
            src[n] = pick(buf, ids_smem[back(n), 0, 0]).astype(BF)
            sel_copy(src, dst, base, n).start()

    def select_fin(buf, src, dst, base, out, size):
        for n in range(1, 8):
            sel_copy(src, dst, base, n).wait_recv()
        total = pick(buf, my_slot)
        for n in (1, 4, 5):
            total = total + dst[n].astype(F32)
        out[0, pl.ds(0, size), :] = total.astype(BF)
        total = dst[2].astype(F32)
        for n in (3, 6, 7):
            total = total + dst[n].astype(F32)
        out[1, pl.ds(0, size), :] = total.astype(BF)
        for n in range(1, 8):
            sel_copy(src, dst, base, n).wait_send()

    def shifted_eye(size, shift):
        row = lax.broadcasted_iota(jnp.int32, (size, 256), 0)
        lane = lax.broadcasted_iota(jnp.int32, (size, 256), 1)
        return jnp.where(lane == row + shift, 1.0, 0.0).astype(BF)

    def build():
        wide = shifted_eye(224, 0)
        place = [shifted_eye(HS, HS * h) for h in range(2)]
        for s in range(4):
            counts = dot_t(fold_ref[...], norms_ref[s].astype(BF)).astype(BF)
            tail = dot(tplace_ref[...], tail_ref[s]).astype(BF)
            entry = dot(counts, nplace_ref[...]) + dot(tail, wide)
            window = sums_ref[546 * s:546 * s + 546, :].astype(BF)
            folded = dot(fslot_ref[...], window).astype(BF)
            for h in range(2):
                entry = entry + dot(folded[h * PF:(h + 1) * PF], place[h])
            ys[y, s] = entry.astype(BF)

    def proj(sh):
        @pl.loop(0, 2)
        def _(c):
            part = pl.ds(pl.multiple_of(c * 256, 256), 256)
            x = xg[0, part, :]
            vqb[sh, part, :] = dot_t(x, lin[sh, 0:256, :]).astype(BF)
            ukb[sh, part, :] = dot_t(x, lin[sh, 256:512, :]).astype(BF)

    def conv(sh):
        vf[pl.ds(0, 16), :] = sfin[sh, PF - 16:PF, :].astype(F32)
        vf[pl.ds(16, LMAX), :] = vqb[sh].astype(F32)
        lane = lax.broadcasted_iota(jnp.int32, (128, 256), 1)
        for n in range(4):
            s = 16 + n * 128
            c = (
                taps[sh, 0:1, :] * vf[s:s + 128, :]
                + taps[sh, 1:2, :] * vf[s - 1:s + 127, :]
                + taps[sh, 2:3, :] * vf[s - 2:s + 126, :]
            )
            u = ukb[sh, n * 128:(n + 1) * 128, :].astype(F32)
            m = c * (u / (1.0 + jnp.exp(-u)))
            m1[sh, n * 128:(n + 1) * 128, :] = jnp.where(lane < 224, m, 1.0).astype(BF)

    def attn(blocks):
        for n in blocks:
            size = 128 * (n + 1)
            lane = lax.broadcasted_iota(jnp.int32, (128, 256), 1)
            row = lax.broadcasted_iota(jnp.int32, (128, size), 0) + n * 128
            col = lax.broadcasted_iota(jnp.int32, (128, size), 1)
            partial = None
            for sh in range(2):
                qb = vqb[sh, n * 128:size, :]
                keys = ukb[sh, 0:size, :]
                mixed = m1[sh, 0:size, :]
                heads = []
                for h in range(2):
                    low = 224 + 16 * h
                    own = jnp.logical_and(lane >= low, lane < low + 16)
                    qh = jnp.where(own, qb.astype(F32), 0.0).astype(BF)
                    a = dot_t(qh, keys) * (FD ** (-0.5))
                    w = jnp.where(col <= row, 1.0 + a + 0.5 * a * a, 0.0).astype(BF)
                    phi = (dot(qb, left_ref[h]) + frow_ref[0:1, :]) * (
                        dot(qb, right_ref[h]) + frow_ref[1:2, :]
                    )
                    phi = (phi * frow_ref[2:3, :]).astype(BF)
                    acc = dot(w, mixed) + dot(phi, sfin[sh])
                    heads.append(acc / acc[:, 224 + h:225 + h])
                out = jnp.where(lane < HS, heads[0], jnp.where(lane < 2 * HS, heads[1], 0.0))
                term = dot(out.astype(BF), lows[sh])
                partial = term if partial is None else partial + term
            pb[n * 128:size, :] = partial.astype(BF)

    def win_proj(c):
        part = slice(c * 256, c * 256 + 256)
        after = slice(c * 256 + WIN, c * 256 + WIN + 256)

        @pl.loop(0, 2)
        def _(sh):
            x = xg[1, part, :]
            qbuf[sh, part, :] = dot_t(x, win[sh, 0:224, :]).astype(BF)
            kbuf[sh, after, :] = dot_t(x, win[sh, 224:448, :]).astype(BF)
            vbuf[sh, after, :] = dot_t(x, win[sh, 448:672, :]).astype(BF)

    def win_prefix():
        for sh in range(2):
            kbuf[sh, pl.ds(0, WIN), :] = kvfin[sh, 0:64, :]
            vbuf[sh, pl.ds(0, WIN), :] = kvfin[sh, 64:128, :]

    def win_attn(blocks):
        lane = lax.broadcasted_iota(jnp.int32, (128, 224), 1)
        row = lax.broadcasted_iota(jnp.int32, (128, 192), 0)
        col = lax.broadcasted_iota(jnp.int32, (128, 192), 1)
        allowed = jnp.logical_and(col > row, col <= row + WIN)
        position = lax.broadcasted_iota(jnp.int32, (128, 1), 0)
        for n in blocks:
            best = None
            partial = None
            for sh in range(2):
                qb = qbuf[sh, n * 128:(n + 1) * 128, :].astype(F32)
                keys = kbuf[sh, n * 128:n * 128 + 192, :]
                vals = vbuf[sh, n * 128:n * 128 + 192, :]
                heads = []
                for h in range(2):
                    own = (lane >= HS) if h else (lane < HS)
                    e = dot_t(jnp.where(own, qb, 0.0).astype(BF), keys) * (HS ** (-0.5))
                    e = jnp.where(allowed, e, -jnp.inf)
                    top = jnp.max(e, axis=-1, keepdims=True)
                    ex = jnp.exp(e - top)
                    p = (ex / jnp.sum(ex, axis=-1, keepdims=True)).astype(BF)
                    heads.append(dot(p, vals))
                    best = top if best is None else jnp.maximum(best, top)
                out = jnp.where(lane < HS, heads[0], heads[1]).astype(BF)
                term = dot(out, win[sh, 672:896, :])
                partial = term if partial is None else partial + term
            hit = jnp.where(position + n * 128 == length - 1, best, -jnp.inf)
            topbuf[n:n + 1, :] = jnp.broadcast_to(jnp.max(hit, axis=0, keepdims=True), (1, 128))
            pb[n * 128:(n + 1) * 128, :] = partial.astype(BF)

    def ffn_in(c):
        @pl.loop(0, 2)
        def _(sh):
            x = xg[2, c * 256:(c + 1) * 256, :]
            for s, e in ((0, 256), (256, 512), (512, 768), (768, 896)):
                g = dot(x, gate[sh, :, s:e])
                u = dot(x, up[sh, :, s:e])
                fbuf[sh, :, s:e] = (g / (1.0 + jnp.exp(-g)) * u).astype(BF)

    def ffn_out(c):
        for s in range(0, D, 256):
            total = dot(fbuf[0], down[0, :, s:s + 256]) + dot(fbuf[1], down[1, :, s:s + 256])
            pb[c * 256:(c + 1) * 256, s:s + 256] = total.astype(BF)

    def last(c):
        x = rs_sum(c).astype(F32)
        place = lax.broadcasted_iota(jnp.int32, (ROWS, 1), 0) + c * 256 + z * ROWS
        x = jnp.where(place < length, x, 0.0)
        ox[c] = x.astype(BF)
        return jnp.sum(jnp.sum(x * x, axis=-1, keepdims=True), axis=0, keepdims=True)

    my_slot = slot_ref[group_ref[xl]]
    length = len_ref[xl]
    info[...] = jnp.full((8, 128), my_slot, jnp.int32)
    build()
    pl.semaphore_wait(barrier, 16)
    y0(ys, 0)
    swap_in().start()
    for n in range(1, 8):
        id_copy(n).start()
    for n in range(4):
        loads[n].wait()
    w0(0)
    first(xl, hidden_ref[xl])
    lows[0, pl.ds(224, 32), :] = jnp.zeros((32, D), BF)
    loads[4].wait()
    w0(5)
    taps[0] = jnp.zeros((8, 256), F32)
    taps[0, 0:3, 0:224] = taps_ref[...]
    tap_swap = remote(taps.at[0], taps.at[1], x_s.at[2], x_r.at[2], d_xp)
    tap_swap.start()
    for sh in range(2):
        sfin[sh, pl.ds(PF, 256 - PF), :] = jnp.zeros((256 - PF, 256), BF)
    topbuf[...] = jnp.full(topbuf.shape, -jnp.inf, F32)
    swap_in().wait_recv()
    first(far_c, hx[...])
    y1(ys, 0)
    for n in range(1, 8):
        id_copy(n).wait_recv()
    to_smem = pltpu.make_async_copy(idr, ids_smem, loc.at[0])
    to_smem.start()
    to_smem.wait()
    ag1(0, xl)
    w1(0)
    ag1(0, far_c)
    yf(ys, 0)
    select_send(ys, sels, rcvs, 8)
    w1(5)
    loads[12].wait()
    loads[13].wait()
    y0(ykv, 6)
    agf(0, 0)
    agf(0, 1)
    for n in range(5, 9):
        loads[n].wait()
    w0(1)
    w2(0)
    proj(0)
    w2(5)
    wf(0)
    y1(ykv, 6)
    for n in range(9, 12):
        loads[n].wait()
    w0(2)
    proj(1)
    tap_swap.wait()
    wf(5)
    select_fin(ys, sels, rcvs, 8, sfin, PF)
    conv(0)
    conv(1)
    attn((0, 1))
    rs0(0)
    w1(1)
    yf(ykv, 6)
    select_send(ykv, selkv, rcvkv, 16)
    w0(3)
    attn((2,))
    rs1(0)
    attn((3,))
    rs0(1)
    w2(1)
    w1(2)
    w0(4)
    rsf(1, 0, g2_ref)
    rs1(1)
    select_fin(ykv, selkv, rcvkv, 16, kvfin, 128)
    win_prefix()
    wf(1)
    ag1(1, 0)
    w1(3)
    rsf(1, 1, g2_ref)
    w2(2)
    agf(1, 0)
    win_proj(0)
    ag1(1, 1)
    win_attn((0, 1))
    rs0(0)
    w1(4)
    w2(3)
    agf(1, 1)
    win_proj(1)
    rs1(0)
    win_attn((2, 3))
    rs0(1)
    rsf(2, 0, g3_ref)
    w2(4)
    rs1(1)
    ag1(2, 0)
    rsf(2, 1, g3_ref)
    agf(2, 0)
    for n in (2, 3, 4):
        wf(n)
    ffn_in(0)
    ag1(2, 1)
    ffn_out(0)
    rs0(0)
    agf(2, 1)
    rs1(0)
    ffn_in(1)
    ffn_out(1)
    rs0(1)
    squares = last(0)
    rs1(1)
    squares = squares + last(1)
    swap_out().start()
    line = lax.broadcasted_iota(jnp.int32, (8, 128), 0)
    top = jnp.max(topbuf[...], axis=0, keepdims=True)
    fins[...] = jnp.where(
        line == xl, squares, jnp.where(line == 2 + xl, top, jnp.where(line < 2, 0.0, -jnp.inf))
    )
    ends = [
        remote(fins, fin.at[k - 1], fin_s.at[k - 1], fin_r.at[k - 1], {"tensor": lax.rem(t + k, 8)})
        for k in range(1, 8)
    ]
    for d in ends:
        d.start()
    out_ref[xl] = ox[xl]
    for d in ends:
        d.wait_recv()
    total = fins[...]
    best = fins[...]
    for k in range(7):
        total = total + fin[k]
        best = jnp.maximum(best, fin[k])
    scal_ref[...] = jnp.where(line < 2, jnp.sqrt(total / D), best)
    swap_out().wait_recv()
    out_ref[far_c] = orx[...]
    swap_out().wait_send()
    swap_in().wait_send()
    for n in range(1, 8):
        id_copy(n).wait_send()
    for d in ends:
        d.wait_send()


def per_device(
    hidden, suffix_len, request_group, group_slot, norm_first, query_weight, key_weight,
    value_weight, filter_gate, filter_taps, linear_out, norm_second, window_query, window_key,
    window_value, window_out, norm_third, gate_weight, up_weight, down_weight, prefix_sums,
    prefix_norms, prefix_keys, prefix_values, prefix_tail,
):
    sums_rows = jnp.transpose(prefix_sums, (0, 2, 1, 3)).reshape(4 * 546, HS)
    vm = pl.BlockSpec(memory_space=pltpu.VMEM)
    hbm = pl.BlockSpec(memory_space=pl.ANY)
    smem = pl.BlockSpec(memory_space=pltpu.SMEM)
    vmem = pltpu.VMEM
    dma = pltpu.SemaphoreType.DMA
    scratch = [vmem((2,) + shape, BF) for shape in SETS] + [
        vmem((3, LMAX, D), BF),
        vmem((LMAX, D), BF),
        vmem((2, 2, ROWS, 896), BF), vmem((2, 2, 2, ROWS, 896), BF),
        vmem((2, ROWS, D), BF), vmem((ROWS, D), BF), vmem((2, ROWS, D), BF), vmem((ROWS, D), BF),
        vmem((4, 4, PF, 256), BF), vmem((4, 4, 128, 224), BF),
        vmem((8, PF, 256), BF), vmem((8, 128, 224), BF),
        vmem((8, PF, 256), BF), vmem((8, 128, 224), BF),
        vmem((2, 256, 256), BF), vmem((2, 128, 224), BF),
        vmem((8, 128), jnp.int32), vmem((8, 8, 128), jnp.int32),
        pltpu.SMEM((8, 8, 128), jnp.int32),
        vmem((2, 8, 256), F32),
        vmem((2, LMAX, 256), BF), vmem((2, LMAX, 256), BF),
        vmem((LMAX + 16, 256), F32), vmem((2, LMAX, 256), BF),
        vmem((2, LMAX, 224), BF), vmem((2, LMAX + WIN, 224), BF), vmem((2, LMAX + WIN, 224), BF),
        vmem((2, 256, FFL), BF),
        vmem((8, 128), F32),
        vmem((7, 8, 128), F32), vmem((8, 128), F32),
        dma((14,)),
        dma((2, 6)), dma((2, 6)), dma((2, 6)), dma((2, 6)),
        dma((12,)), dma((12,)), dma((24,)), dma((24,)),
        dma((6, 6)), dma((6, 6)), dma((3,)), dma((3,)), dma((7,)), dma((7,)), dma((1,)),
    ]
    out, scal = pl.pallas_call(
        kernel,
        out_shape=(
            jax.ShapeDtypeStruct((2, ROWS, D), BF),
            jax.ShapeDtypeStruct((8, 128), F32),
        ),
        in_specs=[smem] * 3 + [vm] * 15 + [hbm] * 14,
        out_specs=(vm, vm),
        scratch_shapes=scratch,
        compiler_params=pltpu.CompilerParams(
            collective_id=0, has_side_effects=True, vmem_limit_bytes=67043328
        ),
        name="layer_pair",
    )(
        request_group, group_slot, suffix_len, hidden, norm_first, norm_second, norm_third,
        filter_taps, sums_rows, prefix_norms, prefix_tail, *constants(),
        prefix_keys, prefix_values, query_weight.T, key_weight.T, value_weight.T,
        filter_gate.T, linear_out, window_query.T, window_key.T, window_value.T, window_out,
        gate_weight, up_weight, down_weight,
    )
    return out, scal[0:2, 0], scal[2:4, 0]


def solution(mesh):
    return jax.shard_map(
        per_device,
        mesh=mesh,
        in_specs=(
            P("req", "tensor", None), P("req"), P("req"), P(), P(),
            P(None, "tensor"), P(None, "tensor"), P(None, "tensor"), P(None, "tensor"),
            P(None, "tensor"), P("tensor", None), P(),
            P(None, "tensor"), P(None, "tensor"), P(None, "tensor"), P("tensor", None), P(),
            P(None, "tensor"), P(None, "tensor"), P("tensor", None),
            P("req", "tensor", None, None), P("req", "tensor", None),
            P("req", None, "tensor"), P("req", None, "tensor"), P("req", None, "tensor"),
        ),
        out_specs=(P("req", "tensor", None), P("req"), P("req")),
        check_vma=False,
    )
```

```python
import jax
import jax.numpy as jnp
import numpy as np
from jax import lax
from jax.experimental import pallas as pl
from jax.experimental.pallas import tpu as pltpu
from jax.sharding import PartitionSpec as P

D = 1792
FD = 16
HS = 112
WIN = 64
LMAX = 512
ROWS = 64
FFL = 896
PF = 160
EPS = 1e-05
BF = jnp.bfloat16
F32 = jnp.float32
MESH = pl.DeviceIdType.MESH
HALVES = ((0, 896), (896, 896))


def constants():
    pairs = [(i, j) for i in range(FD) for j in range(i, FD)]
    fold = np.zeros((PF, 273), np.float32)
    left = np.zeros((2, 256, 256), np.float32)
    right = np.zeros((2, 256, 256), np.float32)
    rows = np.zeros((8, 256), np.float32)
    fold[0, 0] = 1.0
    rows[0, 0] = 1.0
    rows[1, 0] = 1.0
    rows[2, 0] = 1.0
    for i in range(FD):
        fold[1 + i, 1 + i] = 1.0
        for h in range(2):
            left[h, 224 + 16 * h + i, 1 + i] = 1.0
        rows[1, 1 + i] = 1.0
        rows[2, 1 + i] = FD ** (-0.25)
    for n, (i, j) in enumerate(pairs):
        fold[17 + n, 17 + FD * i + j] = 1.0
        fold[17 + n, 17 + FD * j + i] = 1.0
        for h in range(2):
            left[h, 224 + 16 * h + i, 17 + n] = 1.0
            right[h, 224 + 16 * h + j, 17 + n] = 1.0
        rows[2, 17 + n] = (2.0 * FD) ** (-0.5)
    norm_place = np.zeros((2, 256), np.float32)
    for h in range(2):
        norm_place[h, 224 + h] = 1.0
    tail_place = np.zeros((PF, 2), np.float32)
    tail_place[158, 0] = 1.0
    tail_place[159, 1] = 1.0
    fold_slots = np.zeros((2 * PF, 546), np.float32)
    for h in range(2):
        fold_slots[h * PF:(h + 1) * PF, h::2] = fold
    return (
        jnp.asarray(fold, BF),
        jnp.asarray(fold_slots, BF),
        jnp.asarray(left, BF),
        jnp.asarray(right, BF),
        jnp.asarray(rows, F32),
        jnp.asarray(norm_place, BF),
        jnp.asarray(tail_place, BF),
    )


def dot(a, b):
    return jnp.dot(a, b, preferred_element_type=F32)


def dot_t(a, b):
    return lax.dot_general(a, b, (((1,), (1,)), ((), ())), preferred_element_type=F32)

SETS = ((512, D), (896, D), (D, FFL), (D, FFL), (FFL, D), (256, D))


def kernel(
    group_ref,
    slot_ref,
    len_ref,
    hidden_ref,
    g1_ref,
    g2_ref,
    g3_ref,
    taps_ref,
    sums_ref,
    norms_ref,
    tail_ref,
    fold_ref,
    fslot_ref,
    left_ref,
    right_ref,
    frow_ref,
    nplace_ref,
    tplace_ref,
    keys_hbm,
    values_hbm,
    qw_hbm,
    kw_hbm,
    vw_hbm,
    uw_hbm,
    lo_hbm,
    wq_hbm,
    wk_hbm,
    wv_hbm,
    wo_hbm,
    gate_hbm,
    up_hbm,
    down_hbm,
    out_ref,
    scal_ref,
    lin,
    win,
    gate,
    up,
    down,
    lows,
    xg,
    pb,
    l0,
    l1,
    res,
    hx,
    ox,
    orx,
    ys,
    ykv,
    sels,
    selkv,
    rcvs,
    rcvkv,
    sfin,
    kvfin,
    info,
    idr,
    ids_smem,
    taps,
    vqb,
    ukb,
    vf,
    m1,
    qbuf,
    kbuf,
    vbuf,
    fbuf,
    topbuf,
    fin,
    fins,
    wsem,
    ag_s,
    ag_r,
    rs_s,
    rs_r,
    pf_s,
    pf_r,
    sel_s,
    sel_r,
    w_s,
    w_r,
    x_s,
    x_r,
    fin_s,
    fin_r,
    loc,
):
    t = lax.axis_index("tensor")
    rq = lax.axis_index("req")
    z = lax.rem(t, 4)
    xl = t // 4
    core = lax.rem(rq, 2)
    y = lax.rem(rq // 2, 4)
    xh = rq // 8
    xx = xh * 2 + xl
    par = lax.rem(y, 2)
    far_c = 1 - xl

    d_zp = {"tensor": xl * 4 + lax.rem(z + 1, 4)}
    d_zm = {"tensor": xl * 4 + lax.rem(z + 3, 4)}
    d_xp = {"tensor": far_c * 4 + z}
    d_yp = {"req": xh * 8 + lax.rem(y + 1, 4) * 2 + core}
    d_ym = {"req": xh * 8 + lax.rem(y + 3, 4) * 2 + core}
    z_p, z_m, z_z = lax.rem(z + 1, 4), lax.rem(z + 3, 4), lax.rem(z + 2, 4)

    def pal(n):
        x2 = lax.rem(xx + n // 2, 4)
        return {
            "req": (x2 // 2) * 8 + y * 2 + lax.rem(core + n % 2, 2),
            "tensor": lax.rem(x2, 2) * 4 + z,
        }

    pals = {n: pal(n) for n in range(1, 8)}

    barrier = pltpu.get_barrier_semaphore()
    for k in range(1, 8):
        pl.semaphore_signal(
            barrier, inc=1, device_id={"tensor": lax.rem(t + k, 8)}, device_id_type=MESH
        )
    for other in [d_yp, d_ym] + list(pals.values()):
        pl.semaphore_signal(barrier, inc=1, device_id=other, device_id_type=MESH)

    local = [
        (vw_hbm, lin.at[0, pl.ds(0, 224)]),
        (qw_hbm, lin.at[0, pl.ds(224, 32)]),
        (uw_hbm, lin.at[0, pl.ds(256, 224)]),
        (kw_hbm, lin.at[0, pl.ds(480, 32)]),
        (lo_hbm, lows.at[0, pl.ds(0, 224)]),
        (wq_hbm, win.at[0, pl.ds(0, 224)]),
        (wk_hbm, win.at[0, pl.ds(224, 224)]),
        (wv_hbm, win.at[0, pl.ds(448, 224)]),
        (wo_hbm, win.at[0, pl.ds(672, 224)]),
        (gate_hbm, gate.at[0]),
        (up_hbm, up.at[0]),
        (down_hbm, down.at[0]),
        (keys_hbm, ykv.at[y, :, pl.ds(0, 64), :]),
        (values_hbm, ykv.at[y, :, pl.ds(64, 64), :]),
    ]
    loads = [pltpu.make_async_copy(src, dst, wsem.at[n]) for n, (src, dst) in enumerate(local)]
    for n in (0, 1, 2, 3, 4, 12, 13, 5, 6, 7, 8, 9, 10, 11):
        loads[n].start()

    def rows(c, b):
        return pl.ds(pl.multiple_of(c * 256 + b * ROWS, ROWS), ROWS)

    def remote(src, dst, ssem, rsem, to):
        return pltpu.make_async_remote_copy(
            src_ref=src, dst_ref=dst, send_sem=ssem, recv_sem=rsem, device_id=to,
            device_id_type=MESH,
        )

    def ag_part(ph, c, n, b, lanes, to):
        ref = xg.at[ph, rows(c, b), pl.ds(*lanes)]
        return remote(ref, ref, ag_s.at[c, n], ag_r.at[c, n], to)

    def ag_sends(ph, c, first_n, end_n):
        plan = (
            (z, HALVES[0], d_zp),
            (z, HALVES[1], d_zm),
            (z, HALVES[1], d_zp),
            (z, HALVES[0], d_zm),
            (z_m, HALVES[0], d_zp),
            (z_p, HALVES[1], d_zm),
        )
        return [ag_part(ph, c, n, *plan[n]) for n in range(first_n, end_n)]

    def ag_waits(ph, c, first_n, end_n):
        got = (
            (z_m, HALVES[0]),
            (z_p, HALVES[1]),
            (z_m, HALVES[1]),
            (z_p, HALVES[0]),
            (z_z, HALVES[0]),
            (z_z, HALVES[1]),
        )
        return [ag_part(ph, c, n, *got[n], d_zp) for n in range(first_n, end_n)]

    def ag0(ph, c):
        for d in ag_sends(ph, c, 0, 4):
            d.start()

    def ag1(ph, c):
        for n in range(2):
            for d in ag_waits(ph, c, n, n + 1):
                d.wait_recv()
            for d in ag_sends(ph, c, n + 4, n + 5):
                d.start()

    def agf(ph, c):
        for d in ag_waits(ph, c, 2, 6):
            d.wait_recv()
        for d in ag_sends(ph, c, 0, 6):
            d.wait_send()

    def rs_parts(c, first_n, end_n):
        plan = (
            (z_z, 0, d_zm, l0.at[c, 0]),
            (z_z, 1, d_zp, l0.at[c, 1]),
            (z_m, 1, d_zm, l1.at[c, 0, 1]),
            (z_p, 0, d_zp, l1.at[c, 1, 0]),
            (z_m, 0, d_zm, l1.at[c, 0, 0]),
            (z_p, 1, d_zp, l1.at[c, 1, 1]),
        )
        out = []
        for n in range(first_n, end_n):
            b, half, to, land = plan[n]
            src = pb.at[rows(c, b), pl.ds(*HALVES[half])]
            out.append(remote(src, land, rs_s.at[c, n], rs_r.at[c, n], to))
        return out

    def rs0(c):
        for d in rs_parts(c, 0, 4):
            d.start()

    def rs1(c):
        for n, b in ((0, z_m), (1, z_p)):
            for d in rs_parts(c, n, n + 1):
                d.wait_recv()
            where = (rows(c, b), pl.ds(*HALVES[n]))
            pb[where] = (pb[where].astype(F32) + l0[c, n].astype(F32)).astype(BF)
            for d in rs_parts(c, n + 4, n + 5):
                d.start()

    def normed(x, g):
        inverse = lax.rsqrt(jnp.mean(x * x, axis=-1, keepdims=True) + EPS)
        return (x * inverse * g[...].reshape(1, D)).astype(BF)

    def rs_sum(c):
        for d in rs_parts(c, 2, 6):
            d.wait_recv()
        parts = []
        for half in range(2):
            where = (rows(c, z), pl.ds(*HALVES[half]))
            total = pb[where].astype(F32) + l1[c, 0, half].astype(F32) + l1[c, 1, half].astype(F32)
            kept = res[c, :, pl.ds(*HALVES[half])].astype(F32)
            parts.append((kept + total).astype(BF))
        for d in rs_parts(c, 0, 6):
            d.wait_send()
        return jnp.concatenate(parts, axis=1)

    def rsf(ph, c, g):
        total = rs_sum(c)
        res[c] = total
        xg[ph, rows(c, z), :] = normed(total.astype(F32), g)
        ag0(ph, c)

    def first(c, x):
        res[c] = x
        xg[0, rows(c, z), :] = normed(x.astype(F32), g1_ref)
        ag0(0, c)

    def swap_in():
        return remote(hidden_ref.at[far_c], hx, x_s.at[0], x_r.at[0], d_xp)

    def swap_out():
        return remote(ox.at[far_c], orx, x_s.at[1], x_r.at[1], d_xp)

    wbufs = (lin, win, gate, up, down, lows)

    def piece(s, which, cc, pp, side, count=1):
        size = SETS[s][0] // 8
        start = (cc * 4 + pp * 2 + side) * size
        return wbufs[s].at[which, pl.ds(pl.multiple_of(start, 16), size * count)]

    def w_copy(s, n, src, dst, to):
        return remote(src, dst, w_s.at[s, n], w_r.at[s, n], to)

    def w_sends(s, n):
        if n == 0:
            return w_copy(s, n, piece(s, 0, core, par, 0), piece(s, 1, core, par, 0), pals[2])
        if n == 1:
            return w_copy(s, n, piece(s, 0, core, par, 1), piece(s, 1, core, par, 1), pals[6])
        if n == 2:
            ref = piece(s, 1, core, par, 0)
            return w_copy(s, n, ref, ref, d_yp)
        if n == 3:
            ref = piece(s, 1, core, par, 1)
            return w_copy(s, n, ref, ref, d_ym)
        ref = piece(s, 1, core, par if n == 4 else 1 - par, 0, 2)
        return w_copy(s, n, ref, ref, pals[1])

    def w_waits(s, n):
        if n < 2:
            ref = piece(s, 1, core, par, n)
        elif n < 4:
            ref = piece(s, 1, core, 1 - par, n - 2)
        else:
            ref = piece(s, 1, 1 - core, par if n == 4 else 1 - par, 0, 2)
        return w_copy(s, n, ref, ref, pals[1])

    def w0(s):
        for n in range(2):
            w_sends(s, n).start()

    def w1(s):
        for n in range(2):
            w_waits(s, n).wait_recv()
            w_sends(s, n + 2).start()
        w_sends(s, 4).start()

    def w2(s):
        for n in range(2, 4):
            w_waits(s, n).wait_recv()
        w_sends(s, 5).start()

    def wf(s):
        for n in range(4, 6):
            w_waits(s, n).wait_recv()
        for n in range(6):
            w_sends(s, n).wait_send()

    def y_sends(buf, base, n):
        owner = (y, y, y, y, lax.rem(y + 3, 4), lax.rem(y + 1, 4))[n]
        ref = buf.at[owner, pl.ds((0, 2, 2, 0, 0, 2)[n], 2)]
        return remote(ref, ref, pf_s.at[base + n], pf_r.at[base + n], d_ym if n % 2 else d_yp)

    def y_waits(buf, base, n):
        before, after, across = lax.rem(y + 3, 4), lax.rem(y + 1, 4), lax.rem(y + 2, 4)
        owner = (before, after, before, after, across, across)[n]
        ref = buf.at[owner, pl.ds((0, 2, 2, 0, 0, 2)[n], 2)]
        return remote(ref, ref, pf_s.at[base + n], pf_r.at[base + n], d_yp)

    def y0(buf, base):
        for n in range(4):
            y_sends(buf, base, n).start()

    def y1(buf, base):
        for n in range(2):
            y_waits(buf, base, n).wait_recv()
            y_sends(buf, base, n + 4).start()

    def yf(buf, base):
        for n in range(2, 6):
            y_waits(buf, base, n).wait_recv()
        for n in range(6):
            y_sends(buf, base, n).wait_send()

    def id_copy(n):
        return remote(info, idr.at[n], sel_s.at[n], sel_r.at[n], pals[n])

    def sel_copy(src, dst, base, n):
        return remote(src.at[n], dst.at[n], sel_s.at[base + n], sel_r.at[base + n], pals[n])

    def back(n):
        return ((4 - n // 2) % 4) * 2 + n % 2

    def pick(buf, sid):
        owner = sid // 4
        mine = jnp.logical_and(owner // 8 == xh, lax.rem(owner, 2) == core)
        flag = jnp.where(mine, 1.0, 0.0).astype(F32)
        return buf[lax.rem(owner // 2, 4), lax.rem(sid, 4)].astype(F32) * flag

    def select_send(buf, src, dst, base):
        for n in (4, 5, 2, 3, 6, 7, 1):
            src[n] = pick(buf, ids_smem[back(n), 0, 0]).astype(BF)
            sel_copy(src, dst, base, n).start()

    def select_fin(buf, src, dst, base, out, size):
        for n in range(1, 8):
            sel_copy(src, dst, base, n).wait_recv()
        total = pick(buf, my_slot)
        for n in (1, 4, 5):
            total = total + dst[n].astype(F32)
        out[0, pl.ds(0, size), :] = total.astype(BF)
        total = dst[2].astype(F32)
        for n in (3, 6, 7):
            total = total + dst[n].astype(F32)
        out[1, pl.ds(0, size), :] = total.astype(BF)
        for n in range(1, 8):
            sel_copy(src, dst, base, n).wait_send()

    def shifted_eye(size, shift):
        row = lax.broadcasted_iota(jnp.int32, (size, 256), 0)
        lane = lax.broadcasted_iota(jnp.int32, (size, 256), 1)
        return jnp.where(lane == row + shift, 1.0, 0.0).astype(BF)

    def build():
        wide = shifted_eye(224, 0)
        place = [shifted_eye(HS, HS * h) for h in range(2)]
        for s in range(4):
            counts = dot_t(fold_ref[...], norms_ref[s].astype(BF)).astype(BF)
            tail = dot(tplace_ref[...], tail_ref[s]).astype(BF)
            entry = dot(counts, nplace_ref[...]) + dot(tail, wide)
            window = sums_ref[546 * s:546 * s + 546, :].astype(BF)
            folded = dot(fslot_ref[...], window).astype(BF)
            for h in range(2):
                entry = entry + dot(folded[h * PF:(h + 1) * PF], place[h])
            ys[y, s] = entry.astype(BF)

    def proj(sh):
        @pl.loop(0, 2)
        def _(c):
            part = pl.ds(pl.multiple_of(c * 256, 256), 256)
            x = xg[0, part, :]
            vqb[sh, part, :] = dot_t(x, lin[sh, 0:256, :]).astype(BF)
            ukb[sh, part, :] = dot_t(x, lin[sh, 256:512, :]).astype(BF)

    def conv(sh):
        vf[pl.ds(0, 16), :] = sfin[sh, PF - 16:PF, :].astype(F32)
        vf[pl.ds(16, LMAX), :] = vqb[sh].astype(F32)
        lane = lax.broadcasted_iota(jnp.int32, (128, 256), 1)
        for n in range(4):
            s = 16 + n * 128
            c = (
                taps[sh, 0:1, :] * vf[s:s + 128, :]
                + taps[sh, 1:2, :] * vf[s - 1:s + 127, :]
                + taps[sh, 2:3, :] * vf[s - 2:s + 126, :]
            )
            u = ukb[sh, n * 128:(n + 1) * 128, :].astype(F32)
            m = c * (u / (1.0 + jnp.exp(-u)))
            m1[sh, n * 128:(n + 1) * 128, :] = jnp.where(lane < 224, m, 1.0).astype(BF)

    def attn(blocks):
        for n in blocks:
            size = 128 * (n + 1)
            lane = lax.broadcasted_iota(jnp.int32, (128, 256), 1)
            row = lax.broadcasted_iota(jnp.int32, (128, size), 0) + n * 128
            col = lax.broadcasted_iota(jnp.int32, (128, size), 1)
            partial = None
            for sh in range(2):
                qb = vqb[sh, n * 128:size, :]
                keys = ukb[sh, 0:size, :]
                mixed = m1[sh, 0:size, :]
                heads = []
                for h in range(2):
                    low = 224 + 16 * h
                    own = jnp.logical_and(lane >= low, lane < low + 16)
                    qh = jnp.where(own, qb.astype(F32), 0.0).astype(BF)
                    a = dot_t(qh, keys) * (FD ** (-0.5))
                    w = jnp.where(col <= row, 1.0 + a + 0.5 * a * a, 0.0).astype(BF)
                    phi = (dot(qb, left_ref[h]) + frow_ref[0:1, :]) * (
                        dot(qb, right_ref[h]) + frow_ref[1:2, :]
                    )
                    phi = (phi * frow_ref[2:3, :]).astype(BF)
                    acc = dot(w, mixed) + dot(phi, sfin[sh])
                    heads.append(acc / acc[:, 224 + h:225 + h])
                out = jnp.where(lane < HS, heads[0], jnp.where(lane < 2 * HS, heads[1], 0.0))
                term = dot(out.astype(BF), lows[sh])
                partial = term if partial is None else partial + term
            pb[n * 128:size, :] = partial.astype(BF)

    def win_proj(c):
        part = slice(c * 256, c * 256 + 256)
        after = slice(c * 256 + WIN, c * 256 + WIN + 256)

        @pl.loop(0, 2)
        def _(sh):
            x = xg[1, part, :]
            qbuf[sh, part, :] = dot_t(x, win[sh, 0:224, :]).astype(BF)
            kbuf[sh, after, :] = dot_t(x, win[sh, 224:448, :]).astype(BF)
            vbuf[sh, after, :] = dot_t(x, win[sh, 448:672, :]).astype(BF)

    def win_prefix():
        for sh in range(2):
            kbuf[sh, pl.ds(0, WIN), :] = kvfin[sh, 0:64, :]
            vbuf[sh, pl.ds(0, WIN), :] = kvfin[sh, 64:128, :]

    def win_attn(blocks):
        lane = lax.broadcasted_iota(jnp.int32, (128, 224), 1)
        row = lax.broadcasted_iota(jnp.int32, (128, 192), 0)
        col = lax.broadcasted_iota(jnp.int32, (128, 192), 1)
        allowed = jnp.logical_and(col > row, col <= row + WIN)
        position = lax.broadcasted_iota(jnp.int32, (128, 1), 0)
        for n in blocks:
            best = None
            partial = None
            for sh in range(2):
                qb = qbuf[sh, n * 128:(n + 1) * 128, :].astype(F32)
                keys = kbuf[sh, n * 128:n * 128 + 192, :]
                vals = vbuf[sh, n * 128:n * 128 + 192, :]
                heads = []
                for h in range(2):
                    own = (lane >= HS) if h else (lane < HS)
                    e = dot_t(jnp.where(own, qb, 0.0).astype(BF), keys) * (HS ** (-0.5))
                    e = jnp.where(allowed, e, -jnp.inf)
                    top = jnp.max(e, axis=-1, keepdims=True)
                    ex = jnp.exp(e - top)
                    p = (ex / jnp.sum(ex, axis=-1, keepdims=True)).astype(BF)
                    heads.append(dot(p, vals))
                    best = top if best is None else jnp.maximum(best, top)
                out = jnp.where(lane < HS, heads[0], heads[1]).astype(BF)
                term = dot(out, win[sh, 672:896, :])
                partial = term if partial is None else partial + term
            hit = jnp.where(position + n * 128 == length - 1, best, -jnp.inf)
            topbuf[n:n + 1, :] = jnp.broadcast_to(jnp.max(hit, axis=0, keepdims=True), (1, 128))
            pb[n * 128:(n + 1) * 128, :] = partial.astype(BF)

    def ffn_in(c):
        @pl.loop(0, 2)
        def _(sh):
            x = xg[2, c * 256:(c + 1) * 256, :]
            for s, e in ((0, 256), (256, 512), (512, 768), (768, 896)):
                g = dot(x, gate[sh, :, s:e])
                u = dot(x, up[sh, :, s:e])
                fbuf[sh, :, s:e] = (g / (1.0 + jnp.exp(-g)) * u).astype(BF)

    def ffn_out(c):
        for s in range(0, D, 256):
            total = dot(fbuf[0], down[0, :, s:s + 256]) + dot(fbuf[1], down[1, :, s:s + 256])
            pb[c * 256:(c + 1) * 256, s:s + 256] = total.astype(BF)

    def last(c):
        x = rs_sum(c).astype(F32)
        place = lax.broadcasted_iota(jnp.int32, (ROWS, 1), 0) + c * 256 + z * ROWS
        x = jnp.where(place < length, x, 0.0)
        ox[c] = x.astype(BF)
        return jnp.sum(jnp.sum(x * x, axis=-1, keepdims=True), axis=0, keepdims=True)

    my_slot = slot_ref[group_ref[xl]]
    length = len_ref[xl]
    info[...] = jnp.full((8, 128), my_slot, jnp.int32)
    build()
    pl.semaphore_wait(barrier, 16)
    y0(ys, 0)
    swap_in().start()
    for n in range(1, 8):
        id_copy(n).start()
    for n in range(4):
        loads[n].wait()
    w0(0)
    first(xl, hidden_ref[xl])
    lows[0, pl.ds(224, 32), :] = jnp.zeros((32, D), BF)
    loads[4].wait()
    w0(5)
    taps[0] = jnp.zeros((8, 256), F32)
    taps[0, 0:3, 0:224] = taps_ref[...]
    tap_swap = remote(taps.at[0], taps.at[1], x_s.at[2], x_r.at[2], d_xp)
    tap_swap.start()
    for sh in range(2):
        sfin[sh, pl.ds(PF, 256 - PF), :] = jnp.zeros((256 - PF, 256), BF)
    topbuf[...] = jnp.full(topbuf.shape, -jnp.inf, F32)
    swap_in().wait_recv()
    first(far_c, hx[...])
    y1(ys, 0)
    for n in range(1, 8):
        id_copy(n).wait_recv()
    to_smem = pltpu.make_async_copy(idr, ids_smem, loc.at[0])
    to_smem.start()
    to_smem.wait()
    ag1(0, xl)
    w1(0)
    ag1(0, far_c)
    yf(ys, 0)
    select_send(ys, sels, rcvs, 8)
    w1(5)
    loads[12].wait()
    loads[13].wait()
    y0(ykv, 6)
    agf(0, 0)
    agf(0, 1)
    for n in range(5, 9):
        loads[n].wait()
    w0(1)
    w2(0)
    proj(0)
    w2(5)
    wf(0)
    y1(ykv, 6)
    for n in range(9, 12):
        loads[n].wait()
    w0(2)
    proj(1)
    tap_swap.wait()
    wf(5)
    select_fin(ys, sels, rcvs, 8, sfin, PF)
    conv(0)
    conv(1)
    attn((0, 1))
    rs0(0)
    w1(1)
    yf(ykv, 6)
    select_send(ykv, selkv, rcvkv, 16)
    w0(3)
    attn((2,))
    rs1(0)
    attn((3,))
    rs0(1)
    rsf(1, 0, g2_ref)
    rs1(1)
    w2(1)
    ag1(1, 0)
    w0(4)
    w1(2)
    rsf(1, 1, g2_ref)
    wf(1)
    agf(1, 0)
    win_proj(0)
    ag1(1, 1)
    select_fin(ykv, selkv, rcvkv, 16, kvfin, 128)
    win_prefix()
    win_attn((0, 1))
    rs0(0)
    w2(2)
    w1(3)
    agf(1, 1)
    win_proj(1)
    rs1(0)
    win_attn((2, 3))
    rs0(1)
    w1(4)
    rsf(2, 0, g3_ref)
    rs1(1)
    w2(3)
    ag1(2, 0)
    rsf(2, 1, g3_ref)
    w2(4)
    agf(2, 0)
    wf(2)
    wf(3)
    ffn_in(0)
    ag1(2, 1)
    wf(4)
    ffn_out(0)
    rs0(0)
    agf(2, 1)
    ffn_in(1)
    rs1(0)
    ffn_out(1)
    rs0(1)
    squares = last(0)
    rs1(1)
    squares = squares + last(1)
    swap_out().start()
    line = lax.broadcasted_iota(jnp.int32, (8, 128), 0)
    top = jnp.max(topbuf[...], axis=0, keepdims=True)
    fins[...] = jnp.where(
        line == xl, squares, jnp.where(line == 2 + xl, top, jnp.where(line < 2, 0.0, -jnp.inf))
    )
    ends = [
        remote(fins, fin.at[k - 1], fin_s.at[k - 1], fin_r.at[k - 1], {"tensor": lax.rem(t + k, 8)})
        for k in range(1, 8)
    ]
    for d in ends:
        d.start()
    out_ref[xl] = ox[xl]
    for d in ends:
        d.wait_recv()
    total = fins[...]
    best = fins[...]
    for k in range(7):
        total = total + fin[k]
        best = jnp.maximum(best, fin[k])
    scal_ref[...] = jnp.where(line < 2, jnp.sqrt(total / D), best)
    swap_out().wait_recv()
    out_ref[far_c] = orx[...]
    swap_out().wait_send()
    swap_in().wait_send()
    for n in range(1, 8):
        id_copy(n).wait_send()
    for d in ends:
        d.wait_send()


def per_device(
    hidden, suffix_len, request_group, group_slot, norm_first, query_weight, key_weight,
    value_weight, filter_gate, filter_taps, linear_out, norm_second, window_query, window_key,
    window_value, window_out, norm_third, gate_weight, up_weight, down_weight, prefix_sums,
    prefix_norms, prefix_keys, prefix_values, prefix_tail,
):
    sums_rows = jnp.transpose(prefix_sums, (0, 2, 1, 3)).reshape(4 * 546, HS)
    vm = pl.BlockSpec(memory_space=pltpu.VMEM)
    hbm = pl.BlockSpec(memory_space=pl.ANY)
    smem = pl.BlockSpec(memory_space=pltpu.SMEM)
    vmem = pltpu.VMEM
    dma = pltpu.SemaphoreType.DMA
    scratch = [vmem((2,) + shape, BF) for shape in SETS] + [
        vmem((3, LMAX, D), BF),
        vmem((LMAX, D), BF),
        vmem((2, 2, ROWS, 896), BF), vmem((2, 2, 2, ROWS, 896), BF),
        vmem((2, ROWS, D), BF), vmem((ROWS, D), BF), vmem((2, ROWS, D), BF), vmem((ROWS, D), BF),
        vmem((4, 4, PF, 256), BF), vmem((4, 4, 128, 224), BF),
        vmem((8, PF, 256), BF), vmem((8, 128, 224), BF),
        vmem((8, PF, 256), BF), vmem((8, 128, 224), BF),
        vmem((2, 256, 256), BF), vmem((2, 128, 224), BF),
        vmem((8, 128), jnp.int32), vmem((8, 8, 128), jnp.int32),
        pltpu.SMEM((8, 8, 128), jnp.int32),
        vmem((2, 8, 256), F32),
        vmem((2, LMAX, 256), BF), vmem((2, LMAX, 256), BF),
        vmem((LMAX + 16, 256), F32), vmem((2, LMAX, 256), BF),
        vmem((2, LMAX, 224), BF), vmem((2, LMAX + WIN, 224), BF), vmem((2, LMAX + WIN, 224), BF),
        vmem((2, 256, FFL), BF),
        vmem((8, 128), F32),
        vmem((7, 8, 128), F32), vmem((8, 128), F32),
        dma((14,)),
        dma((2, 6)), dma((2, 6)), dma((2, 6)), dma((2, 6)),
        dma((12,)), dma((12,)), dma((24,)), dma((24,)),
        dma((6, 6)), dma((6, 6)), dma((3,)), dma((3,)), dma((7,)), dma((7,)), dma((1,)),
    ]
    out, scal = pl.pallas_call(
        kernel,
        out_shape=(
            jax.ShapeDtypeStruct((2, ROWS, D), BF),
            jax.ShapeDtypeStruct((8, 128), F32),
        ),
        in_specs=[smem] * 3 + [vm] * 15 + [hbm] * 14,
        out_specs=(vm, vm),
        scratch_shapes=scratch,
        compiler_params=pltpu.CompilerParams(
            collective_id=0, has_side_effects=True, vmem_limit_bytes=67043328
        ),
        name="layer_pair",
    )(
        request_group, group_slot, suffix_len, hidden, norm_first, norm_second, norm_third,
        filter_taps, sums_rows, prefix_norms, prefix_tail, *constants(),
        prefix_keys, prefix_values, query_weight.T, key_weight.T, value_weight.T,
        filter_gate.T, linear_out, window_query.T, window_key.T, window_value.T, window_out,
        gate_weight, up_weight, down_weight,
    )
    return out, scal[0:2, 0], scal[2:4, 0]


def solution(mesh):
    return jax.shard_map(
        per_device,
        mesh=mesh,
        in_specs=(
            P("req", "tensor", None), P("req"), P("req"), P(), P(),
            P(None, "tensor"), P(None, "tensor"), P(None, "tensor"), P(None, "tensor"),
            P(None, "tensor"), P("tensor", None), P(),
            P(None, "tensor"), P(None, "tensor"), P(None, "tensor"), P("tensor", None), P(),
            P(None, "tensor"), P(None, "tensor"), P("tensor", None),
            P("req", "tensor", None, None), P("req", "tensor", None),
            P("req", None, "tensor"), P("req", None, "tensor"), P("req", None, "tensor"),
        ),
        out_specs=(P("req", "tensor", None), P("req"), P("req")),
        check_vma=False,
    )
```
